32 devices in a mesh: rows: 2 (over y), cols: 16 (over z, x, core).
Axes of the slice: x: 2, y: 2, z: 4, core: 2. Of those that a mesh axis runs over, the one named last changes fastest.
Arguments:
- eigvecs: float32 [1024, 2048], P('rows', 'cols'), may hold values from -6 to 6
- wy_packed: float32 [32, 128, 128], P(('rows', 'cols')), may hold values from -6 to 6
- slot_block: int32 [2, 8, 2], P('rows'), may hold values from 0 to 1, each once within a row
Outputs:
- transformed: float32 [1024, 2048], P('rows', 'cols')
The draws below stay inside these ranges and needn't reach their ends.
Inputs may be any that keep to these rules, and one draw needn't show every extreme that they name: `slot_block`: for every group and level the 2 entries name each of 0 .. 1 once.
All inputs are finite; a program needn't handle non-finite values.
Results may differ from the reference program's by a relative error of at most 0.0003.
Values sent between devices are 32-bit elements; how exact they have to be, the bound alone decides.
A program may use at most 64 MiB of HBM per device.

```python
import jax
import jax.numpy as jnp
from jax import lax

BAND = 128
LEVELS = 8
HALF = 2
BLOCKS = 32
ROWS = 1024
COLS = 2048
N_ROWS = 2


def steps_of(own_key, dims, split, least, largest):
    loudness = 1.0
    for axis_at, parts in split:
        steps = jax.random.uniform(jax.random.fold_in(jax.random.fold_in(own_key, 6), axis_at), (parts,), jnp.float32, least / len(split), largest / len(split))
        loudness = loudness * jnp.repeat(jnp.exp(steps), dims[axis_at] // parts).reshape((-1,) + (1,) * (len(dims) - 1 - axis_at))
    return loudness


def normal_values(own_key, dims, spread, most, cuts=(), kind=jnp.bfloat16):
    values = jax.random.normal(own_key, dims, jnp.float32) * spread
    if len(cuts) > 0:
        values = steps_of(own_key, dims, cuts, -0.22, 0.18) * values
    return jnp.clip(values, min=-most, max=most).astype(kind)


def setup_inputs(seed: int = 0) -> dict:
    seeds = jax.random.split(jax.random.key(seed), 4)
    eigvecs = normal_values(seeds[0], (ROWS, COLS), 1.0, 6.0, ((0, 2), (1, 16)), jnp.float32)
    wy_packed = normal_values(seeds[1], (BLOCKS, BAND, BAND), 1.0, 6.0, ((0, 32),), jnp.float32)
    slot_block = jax.vmap(lambda own: jax.random.permutation(own, HALF))(jax.random.split(seeds[2], N_ROWS * LEVELS)).reshape((N_ROWS, LEVELS, HALF)).astype(jnp.int32)
    return dict(eigvecs=eigvecs, wy_packed=wy_packed, slot_block=slot_block)


highest = lax.Precision.HIGHEST


def unpack(packed):
    blocks, band_width = packed.shape[0], packed.shape[1]
    flipped = jnp.swapaxes(packed, 1, 2)
    padded = jnp.pad(flipped, ((0, 0), (0, 0), (0, band_width + 1)))
    flattened = padded.reshape(blocks, band_width * (2 * band_width + 1))[:, : 2 * band_width * band_width]
    return flattened.reshape(blocks, band_width, 2 * band_width)


def upper_inverse(upper):
    band_width = upper.shape[1]
    index_row = jnp.arange(band_width, dtype=jnp.int32)
    diag_values = jnp.diagonal(upper, axis1=1, axis2=2)
    identity = jnp.eye(band_width, dtype=upper.dtype)
    inverted = identity[None] * (1.0 / diag_values)[:, None, :]
    width = 1
    while width < band_width:
        same_new = (index_row[:, None] // (2 * width)) == (index_row[None, :] // (2 * width))
        same_old = (index_row[:, None] // width) == (index_row[None, :] // width)
        selector = jnp.logical_and(same_new, jnp.logical_not(same_old)).astype(upper.dtype)
        corner = upper * selector[None]
        partial_block = jnp.einsum("nij,njk->nik", corner, inverted, precision=highest)
        inverted = inverted - jnp.einsum("nij,njk->nik", inverted, partial_block, precision=highest)
        width = 2 * width
    return inverted


def wy_factor(reflectors):
    band_width = reflectors.shape[1]
    gram_matrix = jnp.einsum("njr,nkr->njk", reflectors, reflectors, precision=highest)
    identity = jnp.eye(band_width, dtype=gram_matrix.dtype)
    triangle = jnp.triu(gram_matrix, 1) + 0.5 * gram_matrix * identity
    return upper_inverse(triangle)


def reflect(reflectors, factors, windows):
    projected = jnp.einsum("njr,nrc->njc", reflectors, windows, precision=highest)
    scaled = jnp.einsum("njk,nkc->njc", factors, projected, precision=highest)
    return windows - jnp.einsum("njr,njc->nrc", reflectors, scaled, precision=highest)


def reference(eigvecs, wy_packed, slot_block):
    band_width = wy_packed.shape[1]
    row_count, col_count = eigvecs.shape
    groups = slot_block.shape[0]
    levels_all = slot_block.shape[1]
    per_level = slot_block.shape[2]
    unpacked = unpack(wy_packed)
    reflectors_all = unpacked.reshape(groups, levels_all, per_level, band_width, 2 * band_width)
    factors_all = wy_factor(unpacked).reshape(groups, levels_all, per_level, band_width, band_width)
    current = eigvecs
    padding = jnp.zeros((band_width, col_count), eigvecs.dtype)
    for level_index in range(levels_all):
        chosen = slot_block[:, level_index].astype(jnp.int32)[:, :, None, None]
        reflectors = jnp.take_along_axis(reflectors_all[:, level_index], chosen, axis=1)
        reflectors = reflectors.reshape(groups * per_level, band_width, 2 * band_width)
        factors = jnp.take_along_axis(factors_all[:, level_index], chosen, axis=1)
        factors = factors.reshape(groups * per_level, band_width, band_width)
        if level_index % 2 == 0:
            windows = current.reshape(groups * per_level, 2 * band_width, col_count)
            current = reflect(reflectors, factors, windows).reshape(row_count, col_count)
        else:
            extended = jnp.concatenate([current[band_width:], padding], axis=0)
            windows = extended.reshape(groups * per_level, 2 * band_width, col_count)
            result = reflect(reflectors, factors, windows).reshape(row_count, col_count)
            current = jnp.concatenate([current[:band_width], result[: row_count - band_width]], axis=0)
    return current
```

```python
import functools

import jax
import jax.numpy as jnp
from jax import lax
from jax.experimental import pallas as pl
from jax.experimental.pallas import tpu as pltpu
from jax.sharding import PartitionSpec as P

MESH = pl.DeviceIdType.MESH
F32 = jnp.float32
BF16 = jnp.bfloat16
NN = (((1,), (0,)), ((), ()))
NT = (((1,), (1,)), ((), ()))


def split(value):
    high = value.astype(BF16)
    low = (value - high.astype(F32)).astype(BF16)
    return high, low


def product(a, b, dims=NN):
    dot = functools.partial(lax.dot_general, dimension_numbers=dims, preferred_element_type=F32)
    if dims == NN:
        stacked = jnp.concatenate([a[0], a[1]], axis=1)
        return dot(stacked, jnp.concatenate([b[0], b[0]], axis=0)) + dot(a[0], b[1])
    return dot(a[0], b[0]) + (dot(a[0], b[1]) + dot(a[1], b[0]))


def inverses(grams, multiply):
    band = grams[0].shape[0]
    row = lax.broadcasted_iota(jnp.int32, (band, band), 0)
    col = lax.broadcasted_iota(jnp.int32, (band, band), 1)
    zero = jnp.zeros((band, band), F32)
    diagonal = row == col
    stricts, found = [], []
    for gram in grams:
        on_diagonal = jnp.where(diagonal, 0.5 * gram, zero)
        by_row = 1.0 / jnp.sum(on_diagonal, axis=1, keepdims=True)
        by_col = 1.0 / jnp.sum(on_diagonal, axis=0, keepdims=True)
        strict = jnp.where(col > row, gram, zero)
        pairs = jnp.where(row // 2 == col // 2, strict, zero)
        stricts.append(strict)
        found.append(jnp.where(diagonal, by_row, zero) - pairs * by_row * by_col)
    width = 2
    while width < band:
        factor = 4 if width * 4 <= band else 2
        wide = width * factor
        inside = (row // wide == col // wide) & (row // width != col // width)
        corners = [jnp.where(inside, strict, zero) for strict in stricts]
        powers = [multiply(a, b) for a, b in zip(found, corners)]
        firsts = [multiply(n, a) for n, a in zip(powers, found)]
        found = [a - b for a, b in zip(found, firsts)]
        if factor == 4:
            squares = [multiply(n, n) for n in powers]
            seconds = [multiply(n, a) for n, a in zip(squares, found)]
            found = [a + b for a, b in zip(found, seconds)]
        width = wide
    return found


def fast(a, b):
    return product(split(a), split(b))


def spread(w):
    band = w.shape[0]
    row = lax.broadcasted_iota(jnp.int32, (band, band), 0)
    col = lax.broadcasted_iota(jnp.int32, (band, band), 1)
    upper = col >= row
    zero = jnp.zeros((band, band), F32)
    return jnp.concatenate([jnp.where(upper, w, zero), jnp.where(upper, zero, w)], axis=1)


def own_blocks(sheared):
    v_parts = [split(spread(w)) for w in sheared]
    grams = [product(v, v, NT) for v in v_parts]
    factors = inverses(grams, fast)
    return [product(split(t), v) for t, v in zip(factors, v_parts)]


def paired_kernel(
    levels, n_z, slot_ref, eig_ref, wy_ref, out_ref,
    raw, vz, xin, xt, ops, flags,
    raw_recv, own_send, relay_send, core_recv, core_send, side_sem, local_sem,
):
    band = wy_ref.shape[1]
    chunks = eig_ref.shape[0] // band
    per_level = chunks // 2
    windows = 2 * per_level
    g = lax.axis_index("rows")
    c = lax.axis_index("cols")
    z, x, k = c // 4, (c // 2) % 2, c % 2
    flip_g, flip_x = 1 - 2 * g, 1 - 2 * x
    p1 = {"rows": g + (1 - k) * flip_g, "cols": c + k * 2 * flip_x}
    p2 = {"rows": g + k * flip_g, "cols": c + (1 - k) * 2 * flip_x}
    core_partner = {"rows": g, "cols": c + 1 - 2 * k}
    row_partner = {"rows": 1 - g, "cols": c}

    def z_mate(zz):
        return {"rows": g, "cols": c + 4 * (zz - z)}

    own = g * levels + z * 2 + x

    local_v = pltpu.make_async_copy(wy_ref.at[0], raw.at[own], local_sem.at[0])
    local_x = pltpu.make_async_copy(eig_ref, xin.at[g], local_sem.at[1])
    local_v.start()
    local_x.start()

    barrier = pltpu.get_barrier_semaphore()
    for d in range(1, n_z):
        pl.semaphore_signal(
            barrier, inc=1, device_id=z_mate((z + d) % n_z), device_id_type=MESH
        )
    for other in (p1, p2, core_partner):
        pl.semaphore_signal(barrier, inc=1, device_id=other, device_id_type=MESH)

    level_row = lax.broadcasted_iota(jnp.int32, (levels, band), 0)
    tile = jnp.zeros((levels, band), F32)
    for level in range(levels):
        tile = jnp.where(level_row == level, slot_ref[0, 0, level].astype(F32), tile)
    flags[g] = tile
    xt[2 * chunks] = jnp.zeros((eig_ref.shape[1], band), F32)

    def remote(src, dst, send, recv, target):
        return pltpu.make_async_remote_copy(
            src_ref=src, dst_ref=dst, send_sem=send, recv_sem=recv,
            device_id=target, device_id_type=MESH,
        )

    def from_own(at, target):
        return remote(wy_ref.at[0], raw.at[own], own_send.at[at], raw_recv.at[own], target)

    def to_z(zz):
        return from_own(zz, z_mate(zz))

    def relay(q, zz, way, target):
        return remote(raw.at[q], raw.at[q], relay_send.at[zz, way], raw_recv.at[q], target)

    def across(q):
        return remote(vz.at[k, q], vz.at[k, q], core_send.at[q], core_recv.at[q], core_partner)

    def flags_across():
        return remote(flags.at[g], flags.at[g], side_sem.at[0, 0], side_sem.at[1, 0], row_partner)

    def x_across():
        return remote(eig_ref, xin.at[g], side_sem.at[0, 1], side_sem.at[1, 1], row_partner)

    pl.semaphore_wait(barrier, n_z + 2)
    for zz in range(n_z - 1, -1, -1):
        @pl.when(zz != z)
        def _():
            to_z(zz).start()
    from_own(n_z, p1).start()
    from_own(n_z + 1, p2).start()
    flags_across().start()
    x_across().start()
    local_v.wait()

    def line(j, carry):
        f1, f2 = j % 2, j // 2
        line_g = g + flip_g * (k * f2 + (1 - k) * f1)
        line_x = x + flip_x * (k * f1 + (1 - k) * f2)
        blocks = [line_g * levels + zz * 2 + line_x for zz in range(n_z)]
        for zz in range(n_z - 1, -1, -1):
            q = blocks[zz]

            @pl.when((j > 0) | (zz != z))
            def _():
                relay(q, zz, 0, p1).wait_recv()

            @pl.when((j == 0) & (zz != z))
            def _():
                relay(q, zz, 0, p1).start()
                relay(q, zz, 1, p2).start()

            @pl.when(j == 1)
            def _():
                relay(q, zz, 2, p2).start()

        sheared = [pltpu.roll(jnp.transpose(raw[q]), 0, 1, stride=1, stride_axis=0) for q in blocks]
        for q, w, zed in zip(blocks, sheared, own_blocks(sheared)):
            vz[k, q, 0] = w
            vz[k, q, 1] = zed[:, :band]
            vz[k, q, 2] = zed[:, band:]
        for q in blocks:
            across(q).start()
        return carry

    lax.fori_loop(0, 4, line, 0)

    local_x.wait()
    x_across().wait_recv()
    flags_across().wait_recv()
    for r in range(2):
        for i in range(chunks):
            xt[r * chunks + i] = jnp.transpose(xin[r, i * band : (i + 1) * band, :])
    for q in range(2 * levels):
        across(q).wait_recv()

    def ready(level, base):
        for r in range(2):
            q = r * levels + level
            first = flags[r, pl.ds(level, 1), :] < 0.5
            a, b = vz[0, q], vz[1, q]
            for h, w in enumerate((jnp.where(first, a, b), jnp.where(first, b, a))):
                v = split(spread(w[0]))
                zed = split(jnp.concatenate([w[1], w[2]], axis=1))
                at = base + r * per_level + h
                ops[at, 0], ops[at, 1] = zed
                ops[at, 2], ops[at, 3] = v

    def reflected(base, shift):
        pairs = [
            jnp.concatenate([xt[2 * i + shift], xt[2 * i + shift + 1]], axis=1)
            for i in range(windows)
        ]
        halves = [split(pair) for pair in pairs]
        projected = [
            split(product(h, (ops[base + i, 0], ops[base + i, 1]), NT))
            for i, h in enumerate(halves)
        ]
        for i, (pair, y) in enumerate(zip(pairs, projected)):
            new = pair - product(y, (ops[base + i, 2], ops[base + i, 3]))
            xt[2 * i + shift] = new[:, :band]
            if 2 * i + shift + 1 < 2 * chunks:
                xt[2 * i + shift + 1] = new[:, band:]

    ready(0, 0)

    def both_levels(at, carry):
        ready(2 * at + 1, windows)
        reflected(0, 0)
        ready((2 * at + 2) % levels, 0)
        reflected(windows, 1)
        return carry

    lax.fori_loop(0, levels // 2, both_levels, 0)

    for i in range(chunks):
        out_ref[i * band : (i + 1) * band, :] = jnp.transpose(xt[g * chunks + i])

    for zz in range(n_z):
        q = own + 2 * (zz - z)

        @pl.when(zz != z)
        def _():
            to_z(zz).wait_send()
            relay(q, zz, 0, p1).wait_send()
            relay(q, zz, 1, p2).wait_send()

        relay(q, zz, 2, p2).wait_send()
    from_own(n_z, p1).wait_send()
    from_own(n_z + 1, p2).wait_send()
    flags_across().wait_send()
    x_across().wait_send()
    for q in range(2 * levels):
        across(q).wait_send()


def paired(n_cols, eigvecs, wy_packed, slot_block):
    band = wy_packed.shape[1]
    rows, cols = eigvecs.shape
    levels, per_level = slot_block.shape[1:]
    n_z = n_cols // 4
    chunks = rows // band
    assert n_cols == levels * per_level and 2 * n_z == levels
    assert wy_packed.shape[0] == 1 and per_level == 2 and chunks == 2 * per_level
    anywhere = pl.BlockSpec(memory_space=pl.ANY)
    dma = pltpu.SemaphoreType.DMA
    return pl.pallas_call(
        functools.partial(paired_kernel, levels, n_z),
        out_shape=jax.ShapeDtypeStruct(eigvecs.shape, F32),
        in_specs=[pl.BlockSpec(memory_space=pltpu.SMEM), anywhere, anywhere],
        out_specs=pl.BlockSpec(memory_space=pltpu.VMEM),
        scratch_shapes=[
            pltpu.VMEM((2 * levels, band, band), F32),
            pltpu.VMEM((2, 2 * levels, 3, band, band), F32),
            pltpu.VMEM((2, rows, cols), F32),
            pltpu.VMEM((2 * chunks + 1, cols, band), F32),
            pltpu.VMEM((4 * per_level, 4, band, 2 * band), BF16),
            pltpu.VMEM((2, levels, band), F32),
            dma((2 * levels,)),
            dma((n_z + 2,)),
            dma((n_z, 3)),
            dma((2 * levels,)),
            dma((2 * levels,)),
            dma((2, 2)),
            dma((2,)),
        ],
        compiler_params=pltpu.CompilerParams(collective_id=0, has_side_effects=True),
    )(jnp.swapaxes(slot_block, 1, 2), eigvecs, wy_packed)


def kernel(
    levels, n_rows, n_z, slot_ref, eig_ref, wy_ref, out_ref,
    wg, xt, ops, half_send, above, up_send, up_recv, down_send, down_recv,
    recv_sem, send_sem, own_sem, up_sem, down_sem, half_sem, side_sem,
):
    band = wy_ref.shape[1]
    chunks = eig_ref.shape[0] // band
    per_level = chunks // 2
    rounds = levels // 2
    g = lax.axis_index("rows")
    c = lax.axis_index("cols")
    z, x, k = c // 4, (c // 2) % 2, c % 2
    x_partner = z * 4 + (1 - x) * 2 + k
    core_partner = z * 4 + x * 2 + (1 - k)
    z_mates = [((z + d) % n_z) * 4 + x * 2 + k for d in range(1, n_z)]
    has_above = g > 0
    has_below = g < n_rows - 1

    barrier = pltpu.get_barrier_semaphore()
    for other in z_mates + [x_partner, core_partner]:
        pl.semaphore_signal(barrier, inc=1, device_id={"cols": other}, device_id_type=MESH)

    @pl.when(has_above)
    def _():
        pl.semaphore_signal(barrier, inc=1, device_id={"rows": g - 1}, device_id_type=MESH)

    @pl.when(has_below)
    def _():
        pl.semaphore_signal(barrier, inc=1, device_id={"rows": g + 1}, device_id_type=MESH)

    def block_copy(block, target, sem):
        return pltpu.make_async_remote_copy(
            src_ref=wg.at[block],
            dst_ref=wg.at[block],
            send_sem=sem,
            recv_sem=recv_sem.at[block],
            device_id={"cols": target},
            device_id_type=MESH,
        )

    def to_x(zz, xx):
        return block_copy(zz * 4 + xx * 2 + k, x_partner, send_sem.at[zz * 2 + xx, 0])

    def to_core(zz, xx):
        return block_copy(zz * 4 + xx * 2 + k, core_partner, send_sem.at[zz * 2 + xx, 1])

    def to_z(zz):
        return block_copy(c, zz * 4 + x * 2 + k, own_sem.at[zz])

    def relay_z(zz):
        @pl.when(z != zz)
        def _():
            to_x(zz, x).wait_recv()
            to_x(zz, x).start()
            to_core(zz, x).start()

    def relay_x(zz):
        to_core(zz, 1 - x).wait_recv()
        to_core(zz, 1 - x).start()

    def wait_core(zz):
        for xx in range(2):
            block_copy(zz * 4 + xx * 2 + 1 - k, core_partner, send_sem.at[0, 0]).wait_recv()

    def row_copy(src, dst, sem, at, target):
        return pltpu.make_async_remote_copy(
            src_ref=src.at[at],
            dst_ref=dst.at[at],
            send_sem=sem.at[0, at],
            recv_sem=sem.at[1, at],
            device_id={"rows": target},
            device_id_type=MESH,
        )

    def go_up(at):
        return row_copy(up_send, up_recv, up_sem, at, g - 1)

    def go_down(at):
        return row_copy(down_send, down_recv, down_sem, at, g + 1)

    half = band // 2

    def half_down(at):
        return pltpu.make_async_remote_copy(
            src_ref=half_send.at[at],
            dst_ref=above.at[at, pl.ds(k * half, half)],
            send_sem=half_sem.at[0, at],
            recv_sem=half_sem.at[1, at],
            device_id={"rows": g + 1},
            device_id_type=MESH,
        )

    def half_side(at):
        return pltpu.make_async_remote_copy(
            src_ref=above.at[at, pl.ds(k * half, half)],
            dst_ref=above.at[at, pl.ds(k * half, half)],
            send_sem=side_sem.at[0, at],
            recv_sem=side_sem.at[1, at],
            device_id={"cols": core_partner},
            device_id_type=MESH,
        )

    def send_half(at):
        level = 2 * at + 1
        first = slot_ref[0, per_level - 1, level] == 0
        rows = pl.ds(k * half, half)
        half_send[at] = jnp.where(
            first, wg[level * per_level, rows], wg[level * per_level + 1, rows]
        )
        half_down(at).start()

    wg[c] = pltpu.roll(jnp.transpose(wy_ref[0]), 0, 1, stride=1, stride_axis=0)
    pl.semaphore_wait(
        barrier, n_z + 1 + has_above.astype(jnp.int32) + has_below.astype(jnp.int32)
    )
    to_x(z, x).start()
    to_core(z, x).start()
    for far in range(n_z - 1, -1, -1):
        @pl.when((far != z) & ((far < z) | (z < 2)))
        def _():
            to_z(far).start()

    @pl.when(jnp.logical_not(has_above))
    def _():
        above[...] = jnp.zeros_like(above)
        down_recv[...] = jnp.zeros_like(down_recv)

    @pl.when(jnp.logical_not(has_below))
    def _():
        up_recv[...] = jnp.zeros_like(up_recv)

    for i in range(chunks):
        xt[i] = jnp.transpose(eig_ref[i * band : (i + 1) * band, :])

    def chosen(level, h):
        first = slot_ref[0, h, level] == 0
        return jnp.where(first, wg[level * per_level], wg[level * per_level + 1])

    def prepare(sheared, places):
        v_parts = [split(spread(w)) for w in sheared]
        grams = [product(v, v, NT) for v in v_parts]
        factors = inverses(grams, fast)
        for place, v, t in zip(places, v_parts, factors):
            z_parts = split(product(split(t), v))
            ops[place, 0] = z_parts[0]
            ops[place, 1] = z_parts[1]
            ops[place, 2] = v[0]
            ops[place, 3] = v[1]

    def reflected(places, pairs):
        halves = [split(pair) for pair in pairs]
        projected = [
            split(product(x, (ops[p, 0], ops[p, 1]), NT)) for p, x in zip(places, halves)
        ]
        return [
            pair - product(y, (ops[p, 2], ops[p, 3]))
            for p, y, pair in zip(places, projected, pairs)
        ]

    def window(top, bottom):
        return jnp.concatenate([top, bottom], axis=1)

    relay_z(0)

    @pl.when(z >= 2)
    def _():
        for far in range(n_z - 1, 2, -1):
            @pl.when(far > z)
            def _():
                to_z(far).start()

    relay_x(0)
    wait_core(0)

    @pl.when(has_below)
    def _():
        send_half(0)

    relay_z(1)
    prepare([chosen(0, 0), chosen(0, 1)], [3, 4])

    def both_levels(at, carry):
        @pl.when(has_above)
        def _():
            half_down(at).wait_recv()
            half_side(at).start()

        upper_new, lower_new = reflected([3, 4], [window(xt[0], xt[1]), window(xt[2], xt[3])])
        xt[0], xt[1] = upper_new[:, :band], upper_new[:, band:]
        xt[2], xt[3] = lower_new[:, :band], lower_new[:, band:]

        @pl.when(has_above)
        def _():
            up_send[at] = xt[0]
            go_up(at).start()

        @pl.when(has_below)
        def _():
            down_send[at] = xt[chunks - 1]
            go_down(at).start()

        @pl.when(at < rounds - 1)
        def _():
            relay_x(at + 1)
            wait_core(at + 1)

            @pl.when(has_below)
            def _():
                send_half(at + 1)

        @pl.when(at < rounds - 2)
        def _():
            relay_z(at + 2)

        @pl.when(has_above)
        def _():
            half_side(at).wait_recv()

        odd, even = 2 * at + 1, (2 * at + 2) % levels
        prepare(
            [chosen(odd, 0), chosen(odd, 1), above[at], chosen(even, 0), chosen(even, 1)],
            [0, 1, 2, 3, 4],
        )

        @pl.when(has_below)
        def _():
            go_up(at).wait_recv()

        @pl.when(has_above)
        def _():
            go_down(at).wait_recv()

        middle, last, first = reflected(
            [0, 1, 2],
            [
                window(xt[1], xt[2]),
                window(xt[chunks - 1], up_recv[at]),
                window(down_recv[at], xt[0]),
            ],
        )
        xt[1], xt[2] = middle[:, :band], middle[:, band:]
        xt[chunks - 1] = last[:, :band]
        xt[0] = jnp.where(has_above, first[:, band:], xt[0])
        return carry

    lax.fori_loop(0, rounds, both_levels, 0)

    for i in range(chunks):
        out_ref[i * band : (i + 1) * band, :] = jnp.transpose(xt[i])

    for zz in range(n_z):
        @pl.when(z != zz)
        def _():
            to_z(zz).wait_send()

    for zz in range(n_z):
        to_x(zz, x).wait_send()
        for xx in range(2):
            to_core(zz, xx).wait_send()
    for at in range(rounds):
        @pl.when(has_above)
        def _():
            go_up(at).wait_send()
            half_side(at).wait_send()

        @pl.when(has_below)
        def _():
            go_down(at).wait_send()
            half_down(at).wait_send()


def per_device(n_rows, n_cols, eigvecs, wy_packed, slot_block):
    if n_rows == 2:
        return paired(n_cols, eigvecs, wy_packed, slot_block)
    band = wy_packed.shape[1]
    rows, cols = eigvecs.shape
    levels, per_level = slot_block.shape[1:]
    n_z = n_cols // 4
    rounds = levels // 2
    assert n_cols == levels * per_level and n_z == rounds
    assert wy_packed.shape[0] == 1 and per_level == 2 and rows == 4 * band
    blocks = pltpu.VMEM((rounds, band, band), F32)
    slots = pltpu.VMEM((rounds, cols, band), F32)
    vmem = pl.BlockSpec(memory_space=pltpu.VMEM)
    in_order = pltpu.SemaphoreType.DMA((2, rounds))
    return pl.pallas_call(
        functools.partial(kernel, levels, n_rows, n_z),
        out_shape=jax.ShapeDtypeStruct(eigvecs.shape, F32),
        in_specs=[pl.BlockSpec(memory_space=pltpu.SMEM), vmem, vmem],
        out_specs=vmem,
        scratch_shapes=[
            pltpu.VMEM((n_cols, band, band), F32),
            pltpu.VMEM((rows // band, cols, band), F32),
            pltpu.VMEM((5, 4, band, 2 * band), BF16),
            pltpu.VMEM((rounds, band // 2, band), F32),
            blocks,
            slots,
            slots,
            slots,
            slots,
            pltpu.SemaphoreType.DMA((n_cols,)),
            pltpu.SemaphoreType.DMA((n_cols // 2, 2)),
            pltpu.SemaphoreType.DMA((n_z,)),
            in_order,
            in_order,
            in_order,
            in_order,
        ],
        compiler_params=pltpu.CompilerParams(collective_id=0, has_side_effects=True),
    )(jnp.swapaxes(slot_block, 1, 2), eigvecs, wy_packed)


def solution(mesh):
    placed = (P("rows", "cols"), P(("rows", "cols"), None, None), P("rows", None, None))
    return jax.shard_map(
        functools.partial(per_device, mesh.shape["rows"], mesh.shape["cols"]),
        mesh=mesh, in_specs=placed, out_specs=P("rows", "cols"), check_vma=False,
    )
```

```python
import functools

import jax
import jax.numpy as jnp
from jax import lax
from jax.experimental import pallas as pl
from jax.experimental.pallas import tpu as pltpu
from jax.sharding import PartitionSpec as P

MESH = pl.DeviceIdType.MESH
F32 = jnp.float32
BF16 = jnp.bfloat16
NN = (((1,), (0,)), ((), ()))
NT = (((1,), (1,)), ((), ()))


def split(value):
    high = value.astype(BF16)
    low = (value - high.astype(F32)).astype(BF16)
    return high, low


def product(a, b, dims=NN):
    dot = functools.partial(lax.dot_general, dimension_numbers=dims, preferred_element_type=F32)
    if dims == NN:
        stacked = jnp.concatenate([a[0], a[1]], axis=1)
        return dot(stacked, jnp.concatenate([b[0], b[0]], axis=0)) + dot(a[0], b[1])
    return dot(a[0], b[0]) + (dot(a[0], b[1]) + dot(a[1], b[0]))


def inverses(grams, multiply):
    band = grams[0].shape[0]
    small = 16
    row = lax.broadcasted_iota(jnp.int32, (band, band), 0)
    col = lax.broadcasted_iota(jnp.int32, (band, band), 1)
    zero = jnp.zeros((band, band), F32)
    upper = col > row
    near = row // small == col // small
    stricts = [jnp.where(upper, gram, zero) for gram in grams]

    at = lax.broadcasted_iota(jnp.int32, (small, band), 0)
    lane = lax.broadcasted_iota(jnp.int32, (small, band), 1)
    first = lane // small * small
    on_diagonal = lane - first == at
    none = jnp.zeros((small, band), F32)

    def gathered(value, index):
        return jnp.take_along_axis(value, index, axis=1)

    def side_by_side(value):
        parts = [value[i : i + small] for i in range(0, band, small)]
        return functools.reduce(jnp.add, parts)

    packed = [side_by_side(jnp.where(near, gram, zero)) for gram in grams]
    scales = [
        2.0 / jnp.sum(jnp.where(on_diagonal, p, none), axis=0, keepdims=True) for p in packed
    ]
    scaled = [
        jnp.where(lane - first > at, p, none) * s for p, s in zip(packed, scales)
    ]
    solved = [jnp.where(on_diagonal, 1.0, none) for _ in grams]
    for m in range(small - 1, 0, -1):
        columns = [gathered(s, first + m) for s in scaled]
        solved = [r - a * r[m : m + 1] for r, a in zip(solved, columns)]
    by_row = [gathered(jnp.broadcast_to(s, (small, band)), first + at) for s in scales]
    solved = [r * s for r, s in zip(solved, by_row)]
    found = [
        jnp.where(near, jnp.concatenate([r] * (band // small), axis=0), zero) for r in solved
    ]

    width = small
    while width < band:
        factor = 2 if band // width % 4 else 4
        wide = width * factor
        inside = (row // wide == col // wide) & (row // width != col // width)
        corners = [jnp.where(inside, strict, zero) for strict in stricts]
        powers = [multiply(a, b) for a, b in zip(found, corners)]
        firsts = [multiply(n, a) for n, a in zip(powers, found)]
        found = [a - b for a, b in zip(found, firsts)]
        if factor == 4:
            squares = [multiply(n, n) for n in powers]
            seconds = [multiply(n, a) for n, a in zip(squares, found)]
            found = [a + b for a, b in zip(found, seconds)]
        width = wide
    return found


def fast(a, b):
    return product(split(a), split(b))


def spread(w):
    band = w.shape[0]
    row = lax.broadcasted_iota(jnp.int32, (band, band), 0)
    col = lax.broadcasted_iota(jnp.int32, (band, band), 1)
    upper = col >= row
    zero = jnp.zeros((band, band), F32)
    return jnp.concatenate([jnp.where(upper, w, zero), jnp.where(upper, zero, w)], axis=1)


def own_blocks(sheared):
    v_parts = [split(spread(w)) for w in sheared]
    grams = [product(v, v, NT) for v in v_parts]
    factors = inverses(grams, fast)
    return [product(split(t), v) for t, v in zip(factors, v_parts)]


def paired_kernel(
    levels, n_z, slot_ref, eig_ref, wy_ref, out_ref,
    raw, vz, xin, xt, ops, flags,
    raw_recv, own_send, relay_send, core_recv, core_send, side_sem, local_sem,
):
    band = wy_ref.shape[1]
    chunks = eig_ref.shape[0] // band
    per_level = chunks // 2
    windows = 2 * per_level
    g = lax.axis_index("rows")
    c = lax.axis_index("cols")
    z, x, k = c // 4, (c // 2) % 2, c % 2
    flip_g, flip_x = 1 - 2 * g, 1 - 2 * x
    p1 = {"rows": 1 - g, "cols": c}
    p2 = {"rows": g, "cols": c + 2 * flip_x}
    core_partner = {"rows": g, "cols": c + 1 - 2 * k}
    row_partner = {"rows": 1 - g, "cols": c}

    def z_mate(zz):
        return {"rows": g, "cols": c + 4 * (zz - z)}

    own = g * levels + z * 2 + x

    local_v = pltpu.make_async_copy(wy_ref.at[0], raw.at[own], local_sem.at[0])
    local_x = pltpu.make_async_copy(eig_ref, xin.at[g], local_sem.at[1])
    local_v.start()
    local_x.start()

    barrier = pltpu.get_barrier_semaphore()
    for d in range(1, n_z):
        pl.semaphore_signal(
            barrier, inc=1, device_id=z_mate((z + d) % n_z), device_id_type=MESH
        )
    for other in (p1, p2, core_partner):
        pl.semaphore_signal(barrier, inc=1, device_id=other, device_id_type=MESH)

    level_row = lax.broadcasted_iota(jnp.int32, (levels, band), 0)
    tile = jnp.zeros((levels, band), F32)
    for level in range(levels):
        tile = jnp.where(level_row == level, slot_ref[0, 0, level].astype(F32), tile)
    flags[g] = tile
    xt[2 * chunks] = jnp.zeros((eig_ref.shape[1], band), F32)

    def remote(src, dst, send, recv, target):
        return pltpu.make_async_remote_copy(
            src_ref=src, dst_ref=dst, send_sem=send, recv_sem=recv,
            device_id=target, device_id_type=MESH,
        )

    def from_own(at, target):
        return remote(wy_ref.at[0], raw.at[own], own_send.at[at], raw_recv.at[own], target)

    def to_z(zz):
        return from_own(zz, z_mate(zz))

    def relay(q, zz, way, target):
        return remote(raw.at[q], raw.at[q], relay_send.at[zz, way], raw_recv.at[q], target)

    def across(q):
        return remote(vz.at[k, q], vz.at[k, q], core_send.at[q], core_recv.at[q], core_partner)

    def flags_across():
        return remote(flags.at[g], flags.at[g], side_sem.at[0, 0], side_sem.at[1, 0], row_partner)

    def x_across():
        return remote(eig_ref, xin.at[g], side_sem.at[0, 1], side_sem.at[1, 1], row_partner)

    pl.semaphore_wait(barrier, n_z + 2)
    for zz in range(n_z - 1, -1, -1):
        @pl.when(zz != z)
        def _():
            to_z(zz).start()
    from_own(n_z, p1).start()
    from_own(n_z + 1, p2).start()
    flags_across().start()
    local_v.wait()

    def line(j, carry):
        f1, f2 = j % 2, j // 2
        line_g = g + flip_g * f1
        line_x = x + flip_x * f2
        blocks = [line_g * levels + zz * 2 + line_x for zz in range(n_z)]
        for zz in range(n_z - 1, -1, -1):
            q = blocks[zz]

            @pl.when((j > 0) | (zz != z))
            def _():
                relay(q, zz, 0, p1).wait_recv()

            @pl.when((j == 0) & (zz != z))
            def _():
                relay(q, zz, 0, p1).start()
                relay(q, zz, 1, p2).start()

            @pl.when(j == 1)
            def _():
                relay(q, zz, 2, p2).start()

        @pl.when(j == 0)
        def _():
            x_across().start()

        sheared = [pltpu.roll(jnp.transpose(raw[q]), 0, 1, stride=1, stride_axis=0) for q in blocks]
        for q, w, zed in zip(blocks, sheared, own_blocks(sheared)):
            vz[k, q, 0] = w
            vz[k, q, 1] = zed[:, :band]
            vz[k, q, 2] = zed[:, band:]
        for q in blocks:
            across(q).start()
        return carry

    lax.fori_loop(0, 4, line, 0)

    local_x.wait()
    x_across().wait_recv()
    flags_across().wait_recv()
    for r in range(2):
        for i in range(chunks):
            xt[r * chunks + i] = jnp.transpose(xin[r, i * band : (i + 1) * band, :])
    for q in range(2 * levels):
        across(q).wait_recv()

    def ready(level, base):
        for r in range(2):
            q = r * levels + level
            first = flags[r, pl.ds(level, 1), :] < 0.5
            a, b = vz[0, q], vz[1, q]
            for h, w in enumerate((jnp.where(first, a, b), jnp.where(first, b, a))):
                v = split(spread(w[0]))
                zed = split(jnp.concatenate([w[1], w[2]], axis=1))
                at = base + r * per_level + h
                ops[at, 0], ops[at, 1] = zed
                ops[at, 2], ops[at, 3] = v

    def reflected(base, shift):
        pairs = [
            jnp.concatenate([xt[2 * i + shift], xt[2 * i + shift + 1]], axis=1)
            for i in range(windows)
        ]
        halves = [split(pair) for pair in pairs]
        projected = [
            split(product(h, (ops[base + i, 0], ops[base + i, 1]), NT))
            for i, h in enumerate(halves)
        ]
        for i, (pair, y) in enumerate(zip(pairs, projected)):
            new = pair - product(y, (ops[base + i, 2], ops[base + i, 3]))
            xt[2 * i + shift] = new[:, :band]
            if 2 * i + shift + 1 < 2 * chunks:
                xt[2 * i + shift + 1] = new[:, band:]

    ready(0, 0)

    def both_levels(at, carry):
        ready(2 * at + 1, windows)
        reflected(0, 0)
        ready((2 * at + 2) % levels, 0)
        reflected(windows, 1)
        return carry

    lax.fori_loop(0, levels // 2, both_levels, 0)

    for i in range(chunks):
        out_ref[i * band : (i + 1) * band, :] = jnp.transpose(xt[g * chunks + i])

    for zz in range(n_z):
        q = own + 2 * (zz - z)

        @pl.when(zz != z)
        def _():
            to_z(zz).wait_send()
            relay(q, zz, 0, p1).wait_send()
            relay(q, zz, 1, p2).wait_send()

        relay(q, zz, 2, p2).wait_send()
    from_own(n_z, p1).wait_send()
    from_own(n_z + 1, p2).wait_send()
    flags_across().wait_send()
    x_across().wait_send()
    for q in range(2 * levels):
        across(q).wait_send()


def paired(n_cols, eigvecs, wy_packed, slot_block):
    band = wy_packed.shape[1]
    rows, cols = eigvecs.shape
    levels, per_level = slot_block.shape[1:]
    n_z = n_cols // 4
    chunks = rows // band
    assert n_cols == levels * per_level and 2 * n_z == levels
    assert wy_packed.shape[0] == 1 and per_level == 2 and chunks == 2 * per_level
    anywhere = pl.BlockSpec(memory_space=pl.ANY)
    dma = pltpu.SemaphoreType.DMA
    return pl.pallas_call(
        functools.partial(paired_kernel, levels, n_z),
        out_shape=jax.ShapeDtypeStruct(eigvecs.shape, F32),
        in_specs=[pl.BlockSpec(memory_space=pltpu.SMEM), anywhere, anywhere],
        out_specs=pl.BlockSpec(memory_space=pltpu.VMEM),
        scratch_shapes=[
            pltpu.VMEM((2 * levels, band, band), F32),
            pltpu.VMEM((2, 2 * levels, 3, band, band), F32),
            pltpu.VMEM((2, rows, cols), F32),
            pltpu.VMEM((2 * chunks + 1, cols, band), F32),
            pltpu.VMEM((4 * per_level, 4, band, 2 * band), BF16),
            pltpu.VMEM((2, levels, band), F32),
            dma((2 * levels,)),
            dma((n_z + 2,)),
            dma((n_z, 3)),
            dma((2 * levels,)),
            dma((2 * levels,)),
            dma((2, 2)),
            dma((2,)),
        ],
        compiler_params=pltpu.CompilerParams(collective_id=0, has_side_effects=True),
    )(jnp.swapaxes(slot_block, 1, 2), eigvecs, wy_packed)


def kernel(
    levels, n_rows, n_z, slot_ref, eig_ref, wy_ref, out_ref,
    wg, xt, ops, half_send, above, up_send, up_recv, down_send, down_recv,
    recv_sem, send_sem, own_sem, up_sem, down_sem, half_sem, side_sem,
):
    band = wy_ref.shape[1]
    chunks = eig_ref.shape[0] // band
    per_level = chunks // 2
    rounds = levels // 2
    g = lax.axis_index("rows")
    c = lax.axis_index("cols")
    z, x, k = c // 4, (c // 2) % 2, c % 2
    x_partner = z * 4 + (1 - x) * 2 + k
    core_partner = z * 4 + x * 2 + (1 - k)
    z_mates = [((z + d) % n_z) * 4 + x * 2 + k for d in range(1, n_z)]
    has_above = g > 0
    has_below = g < n_rows - 1

    barrier = pltpu.get_barrier_semaphore()
    for other in z_mates + [x_partner, core_partner]:
        pl.semaphore_signal(barrier, inc=1, device_id={"cols": other}, device_id_type=MESH)

    @pl.when(has_above)
    def _():
        pl.semaphore_signal(barrier, inc=1, device_id={"rows": g - 1}, device_id_type=MESH)

    @pl.when(has_below)
    def _():
        pl.semaphore_signal(barrier, inc=1, device_id={"rows": g + 1}, device_id_type=MESH)

    def block_copy(block, target, sem):
        return pltpu.make_async_remote_copy(
            src_ref=wg.at[block],
            dst_ref=wg.at[block],
            send_sem=sem,
            recv_sem=recv_sem.at[block],
            device_id={"cols": target},
            device_id_type=MESH,
        )

    def to_x(zz, xx):
        return block_copy(zz * 4 + xx * 2 + k, x_partner, send_sem.at[zz * 2 + xx, 0])

    def to_core(zz, xx):
        return block_copy(zz * 4 + xx * 2 + k, core_partner, send_sem.at[zz * 2 + xx, 1])

    def to_z(zz):
        return block_copy(c, zz * 4 + x * 2 + k, own_sem.at[zz])

    def relay_z(zz):
        @pl.when(z != zz)
        def _():
            to_x(zz, x).wait_recv()
            to_x(zz, x).start()
            to_core(zz, x).start()

    def relay_x(zz):
        to_core(zz, 1 - x).wait_recv()
        to_core(zz, 1 - x).start()

    def wait_core(zz):
        for xx in range(2):
            block_copy(zz * 4 + xx * 2 + 1 - k, core_partner, send_sem.at[0, 0]).wait_recv()

    def row_copy(src, dst, sem, at, target):
        return pltpu.make_async_remote_copy(
            src_ref=src.at[at],
            dst_ref=dst.at[at],
            send_sem=sem.at[0, at],
            recv_sem=sem.at[1, at],
            device_id={"rows": target},
            device_id_type=MESH,
        )

    def go_up(at):
        return row_copy(up_send, up_recv, up_sem, at, g - 1)

    def go_down(at):
        return row_copy(down_send, down_recv, down_sem, at, g + 1)

    half = band // 2

    def half_down(at):
        return pltpu.make_async_remote_copy(
            src_ref=half_send.at[at],
            dst_ref=above.at[at, pl.ds(k * half, half)],
            send_sem=half_sem.at[0, at],
            recv_sem=half_sem.at[1, at],
            device_id={"rows": g + 1},
            device_id_type=MESH,
        )

    def half_side(at):
        return pltpu.make_async_remote_copy(
            src_ref=above.at[at, pl.ds(k * half, half)],
            dst_ref=above.at[at, pl.ds(k * half, half)],
            send_sem=side_sem.at[0, at],
            recv_sem=side_sem.at[1, at],
            device_id={"cols": core_partner},
            device_id_type=MESH,
        )

    def send_half(at):
        level = 2 * at + 1
        first = slot_ref[0, per_level - 1, level] == 0
        rows = pl.ds(k * half, half)
        half_send[at] = jnp.where(
            first, wg[level * per_level, rows], wg[level * per_level + 1, rows]
        )
        half_down(at).start()

    wg[c] = pltpu.roll(jnp.transpose(wy_ref[0]), 0, 1, stride=1, stride_axis=0)
    pl.semaphore_wait(
        barrier, n_z + 1 + has_above.astype(jnp.int32) + has_below.astype(jnp.int32)
    )
    to_x(z, x).start()
    to_core(z, x).start()
    for far in range(n_z - 1, -1, -1):
        @pl.when((far != z) & ((far < z) | (z < 2)))
        def _():
            to_z(far).start()

    @pl.when(jnp.logical_not(has_above))
    def _():
        above[...] = jnp.zeros_like(above)
        down_recv[...] = jnp.zeros_like(down_recv)

    @pl.when(jnp.logical_not(has_below))
    def _():
        up_recv[...] = jnp.zeros_like(up_recv)

    for i in range(chunks):
        xt[i] = jnp.transpose(eig_ref[i * band : (i + 1) * band, :])

    def chosen(level, h):
        first = slot_ref[0, h, level] == 0
        return jnp.where(first, wg[level * per_level], wg[level * per_level + 1])

    def prepare(sheared, places):
        v_parts = [split(spread(w)) for w in sheared]
        grams = [product(v, v, NT) for v in v_parts]
        factors = inverses(grams, fast)
        for place, v, t in zip(places, v_parts, factors):
            z_parts = split(product(split(t), v))
            ops[place, 0] = z_parts[0]
            ops[place, 1] = z_parts[1]
            ops[place, 2] = v[0]
            ops[place, 3] = v[1]

    def reflected(places, pairs):
        halves = [split(pair) for pair in pairs]
        projected = [
            split(product(x, (ops[p, 0], ops[p, 1]), NT)) for p, x in zip(places, halves)
        ]
        return [
            pair - product(y, (ops[p, 2], ops[p, 3]))
            for p, y, pair in zip(places, projected, pairs)
        ]

    def window(top, bottom):
        return jnp.concatenate([top, bottom], axis=1)

    relay_z(0)

    @pl.when(z >= 2)
    def _():
        for far in range(n_z - 1, 2, -1):
            @pl.when(far > z)
            def _():
                to_z(far).start()

    relay_x(0)
    wait_core(0)

    @pl.when(has_below)
    def _():
        send_half(0)

    relay_z(1)
    prepare([chosen(0, 0), chosen(0, 1)], [3, 4])

    def both_levels(at, carry):
        @pl.when(has_above)
        def _():
            half_down(at).wait_recv()
            half_side(at).start()

        upper_new, lower_new = reflected([3, 4], [window(xt[0], xt[1]), window(xt[2], xt[3])])
        xt[0], xt[1] = upper_new[:, :band], upper_new[:, band:]
        xt[2], xt[3] = lower_new[:, :band], lower_new[:, band:]

        @pl.when(has_above)
        def _():
            up_send[at] = xt[0]
            go_up(at).start()

        @pl.when(has_below)
        def _():
            down_send[at] = xt[chunks - 1]
            go_down(at).start()

        @pl.when(at < rounds - 1)
        def _():
            relay_x(at + 1)
            wait_core(at + 1)

            @pl.when(has_below)
            def _():
                send_half(at + 1)

        @pl.when(at < rounds - 2)
        def _():
            relay_z(at + 2)

        @pl.when(has_above)
        def _():
            half_side(at).wait_recv()

        odd, even = 2 * at + 1, (2 * at + 2) % levels
        prepare(
            [chosen(odd, 0), chosen(odd, 1), above[at], chosen(even, 0), chosen(even, 1)],
            [0, 1, 2, 3, 4],
        )

        @pl.when(has_below)
        def _():
            go_up(at).wait_recv()

        @pl.when(has_above)
        def _():
            go_down(at).wait_recv()

        middle, last, first = reflected(
            [0, 1, 2],
            [
                window(xt[1], xt[2]),
                window(xt[chunks - 1], up_recv[at]),
                window(down_recv[at], xt[0]),
            ],
        )
        xt[1], xt[2] = middle[:, :band], middle[:, band:]
        xt[chunks - 1] = last[:, :band]
        xt[0] = jnp.where(has_above, first[:, band:], xt[0])
        return carry

    lax.fori_loop(0, rounds, both_levels, 0)

    for i in range(chunks):
        out_ref[i * band : (i + 1) * band, :] = jnp.transpose(xt[i])

    for zz in range(n_z):
        @pl.when(z != zz)
        def _():
            to_z(zz).wait_send()

    for zz in range(n_z):
        to_x(zz, x).wait_send()
        for xx in range(2):
            to_core(zz, xx).wait_send()
    for at in range(rounds):
        @pl.when(has_above)
        def _():
            go_up(at).wait_send()
            half_side(at).wait_send()

        @pl.when(has_below)
        def _():
            go_down(at).wait_send()
            half_down(at).wait_send()


def per_device(n_rows, n_cols, eigvecs, wy_packed, slot_block):
    if n_rows == 2:
        return paired(n_cols, eigvecs, wy_packed, slot_block)
    band = wy_packed.shape[1]
    rows, cols = eigvecs.shape
    levels, per_level = slot_block.shape[1:]
    n_z = n_cols // 4
    rounds = levels // 2
    assert n_cols == levels * per_level and n_z == rounds
    assert wy_packed.shape[0] == 1 and per_level == 2 and rows == 4 * band
    blocks = pltpu.VMEM((rounds, band, band), F32)
    slots = pltpu.VMEM((rounds, cols, band), F32)
    vmem = pl.BlockSpec(memory_space=pltpu.VMEM)
    in_order = pltpu.SemaphoreType.DMA((2, rounds))
    return pl.pallas_call(
        functools.partial(kernel, levels, n_rows, n_z),
        out_shape=jax.ShapeDtypeStruct(eigvecs.shape, F32),
        in_specs=[pl.BlockSpec(memory_space=pltpu.SMEM), vmem, vmem],
        out_specs=vmem,
        scratch_shapes=[
            pltpu.VMEM((n_cols, band, band), F32),
            pltpu.VMEM((rows // band, cols, band), F32),
            pltpu.VMEM((5, 4, band, 2 * band), BF16),
            pltpu.VMEM((rounds, band // 2, band), F32),
            blocks,
            slots,
            slots,
            slots,
            slots,
            pltpu.SemaphoreType.DMA((n_cols,)),
            pltpu.SemaphoreType.DMA((n_cols // 2, 2)),
            pltpu.SemaphoreType.DMA((n_z,)),
            in_order,
            in_order,
            in_order,
            in_order,
        ],
        compiler_params=pltpu.CompilerParams(collective_id=0, has_side_effects=True),
    )(jnp.swapaxes(slot_block, 1, 2), eigvecs, wy_packed)


def solution(mesh):
    placed = (P("rows", "cols"), P(("rows", "cols"), None, None), P("rows", None, None))
    return jax.shard_map(
        functools.partial(per_device, mesh.shape["rows"], mesh.shape["cols"]),
        mesh=mesh, in_specs=placed, out_specs=P("rows", "cols"), check_vma=False,
    )
```

```python
import functools

import jax
import jax.numpy as jnp
from jax import lax
from jax.experimental import pallas as pl
from jax.experimental.pallas import tpu as pltpu
from jax.sharding import PartitionSpec as P

MESH = pl.DeviceIdType.MESH
F32 = jnp.float32
BF16 = jnp.bfloat16
NN = (((1,), (0,)), ((), ()))
NT = (((1,), (1,)), ((), ()))


def split(value):
    high = value.astype(BF16)
    low = (value - high.astype(F32)).astype(BF16)
    return high, low


def product(a, b, dims=NN):
    dot = functools.partial(lax.dot_general, dimension_numbers=dims, preferred_element_type=F32)
    if dims == NN:
        stacked = jnp.concatenate([a[0], a[1]], axis=1)
        return dot(stacked, jnp.concatenate([b[0], b[0]], axis=0)) + dot(a[0], b[1])
    return dot(a[0], b[0]) + (dot(a[0], b[1]) + dot(a[1], b[0]))


def inverses(grams, multiply):
    band = grams[0].shape[0]
    small = 16
    row = lax.broadcasted_iota(jnp.int32, (band, band), 0)
    col = lax.broadcasted_iota(jnp.int32, (band, band), 1)
    zero = jnp.zeros((band, band), F32)
    upper = col > row
    near = row // small == col // small
    stricts = [jnp.where(upper, gram, zero) for gram in grams]

    at = lax.broadcasted_iota(jnp.int32, (small, band), 0)
    lane = lax.broadcasted_iota(jnp.int32, (small, band), 1)
    first = lane // small * small
    on_diagonal = lane - first == at
    none = jnp.zeros((small, band), F32)

    def gathered(value, index):
        return jnp.take_along_axis(value, index, axis=1)

    def side_by_side(value):
        parts = [value[i : i + small] for i in range(0, band, small)]
        return functools.reduce(jnp.add, parts)

    packed = [side_by_side(jnp.where(near, gram, zero)) for gram in grams]
    scales = [
        2.0 / jnp.sum(jnp.where(on_diagonal, p, none), axis=0, keepdims=True) for p in packed
    ]
    scaled = [
        jnp.where(lane - first > at, p, none) * s for p, s in zip(packed, scales)
    ]
    solved = [jnp.where(on_diagonal, 1.0, none) for _ in grams]
    for m in range(small - 1, 0, -1):
        columns = [gathered(s, first + m) for s in scaled]
        solved = [r - a * r[m : m + 1] for r, a in zip(solved, columns)]
    by_row = [gathered(jnp.broadcast_to(s, (small, band)), first + at) for s in scales]
    solved = [r * s for r, s in zip(solved, by_row)]
    found = [
        jnp.where(near, jnp.concatenate([r] * (band // small), axis=0), zero) for r in solved
    ]

    width = small
    while width < band:
        factor = 2 if band // width % 4 else 4
        wide = width * factor
        inside = (row // wide == col // wide) & (row // width != col // width)
        corners = [jnp.where(inside, strict, zero) for strict in stricts]
        powers = [multiply(a, b) for a, b in zip(found, corners)]
        firsts = [multiply(n, a) for n, a in zip(powers, found)]
        found = [a - b for a, b in zip(found, firsts)]
        if factor == 4:
            squares = [multiply(n, n) for n in powers]
            seconds = [multiply(n, a) for n, a in zip(squares, found)]
            found = [a + b for a, b in zip(found, seconds)]
        width = wide
    return found


def fast(a, b):
    return product(split(a), split(b))


def spread(w):
    band = w.shape[0]
    row = lax.broadcasted_iota(jnp.int32, (band, band), 0)
    col = lax.broadcasted_iota(jnp.int32, (band, band), 1)
    upper = col >= row
    zero = jnp.zeros((band, band), F32)
    return jnp.concatenate([jnp.where(upper, w, zero), jnp.where(upper, zero, w)], axis=1)


def own_blocks(sheared):
    v_parts = [split(spread(w)) for w in sheared]
    grams = [product(v, v, NT) for v in v_parts]
    factors = inverses(grams, fast)
    return [product(split(t), v) for t, v in zip(factors, v_parts)]


def paired_kernel(
    levels, n_z, slot_ref, eig_ref, wy_ref, out_ref,
    raw, vz, xin, xt, ops, flags,
    raw_recv, own_send, relay_send, core_recv, core_send, side_sem, local_sem,
):
    band = wy_ref.shape[1]
    chunks = eig_ref.shape[0] // band
    per_level = chunks // 2
    windows = 2 * per_level
    g = lax.axis_index("rows")
    c = lax.axis_index("cols")
    z, x, k = c // 4, (c // 2) % 2, c % 2
    flip_g, flip_x = 1 - 2 * g, 1 - 2 * x
    p1 = {"rows": 1 - g, "cols": c}
    p2 = {"rows": g, "cols": c + 2 * flip_x}
    p3 = {"rows": 1 - g, "cols": c + 2 * flip_x}
    core_partner = {"rows": g, "cols": c + 1 - 2 * k}
    row_partner = {"rows": 1 - g, "cols": c}

    def z_mate(zz):
        return {"rows": g, "cols": c + 4 * (zz - z)}

    own = g * levels + z * 2 + x
    opposite = (1 - g) * levels + z * 2 + 1 - x

    local_v = pltpu.make_async_copy(wy_ref.at[0], raw.at[own], local_sem.at[0])
    local_x = pltpu.make_async_copy(eig_ref, xin.at[g], local_sem.at[1])
    local_v.start()
    local_x.start()

    barrier = pltpu.get_barrier_semaphore()
    for d in range(1, n_z):
        pl.semaphore_signal(
            barrier, inc=1, device_id=z_mate((z + d) % n_z), device_id_type=MESH
        )
    for other in (p1, p2, p3, core_partner):
        pl.semaphore_signal(barrier, inc=1, device_id=other, device_id_type=MESH)

    level_row = lax.broadcasted_iota(jnp.int32, (levels, band), 0)
    tile = jnp.zeros((levels, band), F32)
    for level in range(levels):
        tile = jnp.where(level_row == level, slot_ref[0, 0, level].astype(F32), tile)
    flags[g] = tile
    xt[2 * chunks] = jnp.zeros((eig_ref.shape[1], band), F32)

    def remote(src, dst, send, recv, target):
        return pltpu.make_async_remote_copy(
            src_ref=src, dst_ref=dst, send_sem=send, recv_sem=recv,
            device_id=target, device_id_type=MESH,
        )

    def from_own(at, target):
        return remote(raw.at[own], raw.at[own], own_send.at[at], raw_recv.at[own], target)

    def to_z(zz):
        return from_own(zz, z_mate(zz))

    def relay(q, zz, way, target):
        return remote(raw.at[q], raw.at[q], relay_send.at[zz, way], raw_recv.at[q], target)

    def across(q):
        return remote(vz.at[k, q], vz.at[k, q], core_send.at[q], core_recv.at[q], core_partner)

    def flags_across():
        return remote(flags.at[g], flags.at[g], side_sem.at[0, 0], side_sem.at[1, 0], row_partner)

    def x_across():
        return remote(eig_ref, xin.at[g], side_sem.at[0, 1], side_sem.at[1, 1], row_partner)

    local_v.wait()
    pl.semaphore_wait(barrier, n_z + 3)

    @pl.when(k == 0)
    def _():
        from_own(n_z + 2, p3).start()

    for zz in range(n_z - 1, -1, -1):
        @pl.when(zz != z)
        def _():
            to_z(zz).start()
    from_own(n_z, p1).start()
    from_own(n_z + 1, p2).start()
    flags_across().start()

    side = jnp.where(z < n_z // 2, 1, n_z - 1)

    def plane(step, carry):
        zz = (z + side * step) % n_z
        at = zz * 2 + x
        mine = g * levels + at
        across_y = (1 - g) * levels + at
        across_x = g * levels + at + flip_x
        across_both = (1 - g) * levels + at + flip_x
        blocks = [mine, across_y, across_x, across_both]

        @pl.when((step == 0) & (k == 0))
        def _():
            relay(across_both, 0, 0, p1).wait_recv()
            for d in range(n_z - 1, 0, -1):
                far = (z + d) % n_z
                relay(opposite, far, 2, z_mate(far)).start()

        @pl.when((step == 0) & (k == 1))
        def _():
            relay(across_y, 0, 0, p1).wait_recv()
            relay(across_y, z, 2, p2).start()

        @pl.when(step == 0)
        def _():
            for d in range(1, n_z):
                far = (z + side * d) % n_z
                q = g * levels + far * 2 + x
                relay(q, far, 0, p1).wait_recv()
                relay(q, far, 0, p1).start()
                relay(q, far, 1, p2).start()
            x_across().start()

        @pl.when(k == 0)
        def _():
            relay(across_y, 0, 0, p1).wait_recv()

        @pl.when((step > 0) | (k == 1))
        def _():
            relay(across_both, 0, 0, p1).wait_recv()

        relay(across_x, 0, 0, p1).wait_recv()
        sheared = [pltpu.roll(jnp.transpose(raw[q]), 0, 1, stride=1, stride_axis=0) for q in blocks]
        for q, w, zed in zip(blocks, sheared, own_blocks(sheared)):
            vz[k, q, 0] = w
            vz[k, q, 1] = zed[:, :band]
            vz[k, q, 2] = zed[:, band:]
        for q in blocks:
            across(q).start()

        @pl.when((step == 0) & (k == 1))
        def _():
            for d in range(1, n_z):
                far = (z + side * d) % n_z
                q = (1 - g) * levels + far * 2 + x
                relay(q, far, 0, p1).wait_recv()
                relay(q, far, 2, p2).start()

        return carry

    lax.fori_loop(0, n_z, plane, 0)

    local_x.wait()
    x_across().wait_recv()
    flags_across().wait_recv()
    for r in range(2):
        for i in range(chunks):
            xt[r * chunks + i] = jnp.transpose(xin[r, i * band : (i + 1) * band, :])
    for q in range(2 * levels):
        across(q).wait_recv()

    def ready(level, base):
        for r in range(2):
            q = r * levels + level
            first = flags[r, pl.ds(level, 1), :] < 0.5
            a, b = vz[0, q], vz[1, q]
            for h, w in enumerate((jnp.where(first, a, b), jnp.where(first, b, a))):
                v = split(spread(w[0]))
                zed = split(jnp.concatenate([w[1], w[2]], axis=1))
                at = base + r * per_level + h
                ops[at, 0], ops[at, 1] = zed
                ops[at, 2], ops[at, 3] = v

    def reflected(base, shift):
        pairs = [
            jnp.concatenate([xt[2 * i + shift], xt[2 * i + shift + 1]], axis=1)
            for i in range(windows)
        ]
        halves = [split(pair) for pair in pairs]
        projected = [
            split(product(h, (ops[base + i, 0], ops[base + i, 1]), NT))
            for i, h in enumerate(halves)
        ]
        for i, (pair, y) in enumerate(zip(pairs, projected)):
            new = pair - product(y, (ops[base + i, 2], ops[base + i, 3]))
            xt[2 * i + shift] = new[:, :band]
            if 2 * i + shift + 1 < 2 * chunks:
                xt[2 * i + shift + 1] = new[:, band:]

    ready(0, 0)

    def both_levels(at, carry):
        ready(2 * at + 1, windows)
        reflected(0, 0)
        ready((2 * at + 2) % levels, 0)
        reflected(windows, 1)
        return carry

    lax.fori_loop(0, levels // 2, both_levels, 0)

    for i in range(chunks):
        out_ref[i * band : (i + 1) * band, :] = jnp.transpose(xt[g * chunks + i])

    for zz in range(n_z):
        q = own + 2 * (zz - z)

        @pl.when(zz != z)
        def _():
            to_z(zz).wait_send()
            relay(q, zz, 0, p1).wait_send()
            relay(q, zz, 1, p2).wait_send()

        @pl.when((zz != z) | (k == 1))
        def _():
            relay(q, zz, 2, p2).wait_send()

    from_own(n_z, p1).wait_send()
    from_own(n_z + 1, p2).wait_send()

    @pl.when(k == 0)
    def _():
        from_own(n_z + 2, p3).wait_send()

    flags_across().wait_send()
    x_across().wait_send()
    for q in range(2 * levels):
        across(q).wait_send()


def paired(n_cols, eigvecs, wy_packed, slot_block):
    band = wy_packed.shape[1]
    rows, cols = eigvecs.shape
    levels, per_level = slot_block.shape[1:]
    n_z = n_cols // 4
    chunks = rows // band
    assert n_cols == levels * per_level and 2 * n_z == levels
    assert wy_packed.shape[0] == 1 and per_level == 2 and chunks == 2 * per_level
    anywhere = pl.BlockSpec(memory_space=pl.ANY)
    dma = pltpu.SemaphoreType.DMA
    return pl.pallas_call(
        functools.partial(paired_kernel, levels, n_z),
        out_shape=jax.ShapeDtypeStruct(eigvecs.shape, F32),
        in_specs=[pl.BlockSpec(memory_space=pltpu.SMEM), anywhere, anywhere],
        out_specs=pl.BlockSpec(memory_space=pltpu.VMEM),
        scratch_shapes=[
            pltpu.VMEM((2 * levels, band, band), F32),
            pltpu.VMEM((2, 2 * levels, 3, band, band), F32),
            pltpu.VMEM((2, rows, cols), F32),
            pltpu.VMEM((2 * chunks + 1, cols, band), F32),
            pltpu.VMEM((4 * per_level, 4, band, 2 * band), BF16),
            pltpu.VMEM((2, levels, band), F32),
            dma((2 * levels,)),
            dma((n_z + 3,)),
            dma((n_z, 3)),
            dma((2 * levels,)),
            dma((2 * levels,)),
            dma((2, 2)),
            dma((2,)),
        ],
        compiler_params=pltpu.CompilerParams(collective_id=0, has_side_effects=True),
    )(jnp.swapaxes(slot_block, 1, 2), eigvecs, wy_packed)


def kernel(
    levels, n_rows, n_z, slot_ref, eig_ref, wy_ref, out_ref,
    wg, xt, ops, half_send, above, up_send, up_recv, down_send, down_recv,
    recv_sem, send_sem, own_sem, up_sem, down_sem, half_sem, side_sem,
):
    band = wy_ref.shape[1]
    chunks = eig_ref.shape[0] // band
    per_level = chunks // 2
    rounds = levels // 2
    g = lax.axis_index("rows")
    c = lax.axis_index("cols")
    z, x, k = c // 4, (c // 2) % 2, c % 2
    x_partner = z * 4 + (1 - x) * 2 + k
    core_partner = z * 4 + x * 2 + (1 - k)
    z_mates = [((z + d) % n_z) * 4 + x * 2 + k for d in range(1, n_z)]
    has_above = g > 0
    has_below = g < n_rows - 1

    barrier = pltpu.get_barrier_semaphore()
    for other in z_mates + [x_partner, core_partner]:
        pl.semaphore_signal(barrier, inc=1, device_id={"cols": other}, device_id_type=MESH)

    @pl.when(has_above)
    def _():
        pl.semaphore_signal(barrier, inc=1, device_id={"rows": g - 1}, device_id_type=MESH)

    @pl.when(has_below)
    def _():
        pl.semaphore_signal(barrier, inc=1, device_id={"rows": g + 1}, device_id_type=MESH)

    def block_copy(block, target, sem):
        return pltpu.make_async_remote_copy(
            src_ref=wg.at[block],
            dst_ref=wg.at[block],
            send_sem=sem,
            recv_sem=recv_sem.at[block],
            device_id={"cols": target},
            device_id_type=MESH,
        )

    def to_x(zz, xx):
        return block_copy(zz * 4 + xx * 2 + k, x_partner, send_sem.at[zz * 2 + xx, 0])

    def to_core(zz, xx):
        return block_copy(zz * 4 + xx * 2 + k, core_partner, send_sem.at[zz * 2 + xx, 1])

    def to_z(zz):
        return block_copy(c, zz * 4 + x * 2 + k, own_sem.at[zz])

    def relay_z(zz):
        @pl.when(z != zz)
        def _():
            to_x(zz, x).wait_recv()
            to_x(zz, x).start()
            to_core(zz, x).start()

    def relay_x(zz):
        to_core(zz, 1 - x).wait_recv()
        to_core(zz, 1 - x).start()

    def wait_core(zz):
        for xx in range(2):
            block_copy(zz * 4 + xx * 2 + 1 - k, core_partner, send_sem.at[0, 0]).wait_recv()

    def row_copy(src, dst, sem, at, target):
        return pltpu.make_async_remote_copy(
            src_ref=src.at[at],
            dst_ref=dst.at[at],
            send_sem=sem.at[0, at],
            recv_sem=sem.at[1, at],
            device_id={"rows": target},
            device_id_type=MESH,
        )

    def go_up(at):
        return row_copy(up_send, up_recv, up_sem, at, g - 1)

    def go_down(at):
        return row_copy(down_send, down_recv, down_sem, at, g + 1)

    half = band // 2

    def half_down(at):
        return pltpu.make_async_remote_copy(
            src_ref=half_send.at[at],
            dst_ref=above.at[at, pl.ds(k * half, half)],
            send_sem=half_sem.at[0, at],
            recv_sem=half_sem.at[1, at],
            device_id={"rows": g + 1},
            device_id_type=MESH,
        )

    def half_side(at):
        return pltpu.make_async_remote_copy(
            src_ref=above.at[at, pl.ds(k * half, half)],
            dst_ref=above.at[at, pl.ds(k * half, half)],
            send_sem=side_sem.at[0, at],
            recv_sem=side_sem.at[1, at],
            device_id={"cols": core_partner},
            device_id_type=MESH,
        )

    def send_half(at):
        level = 2 * at + 1
        first = slot_ref[0, per_level - 1, level] == 0
        rows = pl.ds(k * half, half)
        half_send[at] = jnp.where(
            first, wg[level * per_level, rows], wg[level * per_level + 1, rows]
        )
        half_down(at).start()

    wg[c] = pltpu.roll(jnp.transpose(wy_ref[0]), 0, 1, stride=1, stride_axis=0)
    pl.semaphore_wait(
        barrier, n_z + 1 + has_above.astype(jnp.int32) + has_below.astype(jnp.int32)
    )
    to_x(z, x).start()
    to_core(z, x).start()
    for far in range(n_z - 1, -1, -1):
        @pl.when((far != z) & ((far < z) | (z < 2)))
        def _():
            to_z(far).start()

    @pl.when(jnp.logical_not(has_above))
    def _():
        above[...] = jnp.zeros_like(above)
        down_recv[...] = jnp.zeros_like(down_recv)

    @pl.when(jnp.logical_not(has_below))
    def _():
        up_recv[...] = jnp.zeros_like(up_recv)

    for i in range(chunks):
        xt[i] = jnp.transpose(eig_ref[i * band : (i + 1) * band, :])

    def chosen(level, h):
        first = slot_ref[0, h, level] == 0
        return jnp.where(first, wg[level * per_level], wg[level * per_level + 1])

    def prepare(sheared, places):
        v_parts = [split(spread(w)) for w in sheared]
        grams = [product(v, v, NT) for v in v_parts]
        factors = inverses(grams, fast)
        for place, v, t in zip(places, v_parts, factors):
            z_parts = split(product(split(t), v))
            ops[place, 0] = z_parts[0]
            ops[place, 1] = z_parts[1]
            ops[place, 2] = v[0]
            ops[place, 3] = v[1]

    def reflected(places, pairs):
        halves = [split(pair) for pair in pairs]
        projected = [
            split(product(x, (ops[p, 0], ops[p, 1]), NT)) for p, x in zip(places, halves)
        ]
        return [
            pair - product(y, (ops[p, 2], ops[p, 3]))
            for p, y, pair in zip(places, projected, pairs)
        ]

    def window(top, bottom):
        return jnp.concatenate([top, bottom], axis=1)

    relay_z(0)

    @pl.when(z >= 2)
    def _():
        for far in range(n_z - 1, 2, -1):
            @pl.when(far > z)
            def _():
                to_z(far).start()

    relay_x(0)
    wait_core(0)

    @pl.when(has_below)
    def _():
        send_half(0)

    relay_z(1)
    prepare([chosen(0, 0), chosen(0, 1)], [3, 4])

    def both_levels(at, carry):
        @pl.when(has_above)
        def _():
            half_down(at).wait_recv()
            half_side(at).start()

        upper_new, lower_new = reflected([3, 4], [window(xt[0], xt[1]), window(xt[2], xt[3])])
        xt[0], xt[1] = upper_new[:, :band], upper_new[:, band:]
        xt[2], xt[3] = lower_new[:, :band], lower_new[:, band:]

        @pl.when(has_above)
        def _():
            up_send[at] = xt[0]
            go_up(at).start()

        @pl.when(has_below)
        def _():
            down_send[at] = xt[chunks - 1]
            go_down(at).start()

        @pl.when(at < rounds - 1)
        def _():
            relay_x(at + 1)
            wait_core(at + 1)

            @pl.when(has_below)
            def _():
                send_half(at + 1)

        @pl.when(at < rounds - 2)
        def _():
            relay_z(at + 2)

        @pl.when(has_above)
        def _():
            half_side(at).wait_recv()

        odd, even = 2 * at + 1, (2 * at + 2) % levels
        prepare(
            [chosen(odd, 0), chosen(odd, 1), above[at], chosen(even, 0), chosen(even, 1)],
            [0, 1, 2, 3, 4],
        )

        @pl.when(has_below)
        def _():
            go_up(at).wait_recv()

        @pl.when(has_above)
        def _():
            go_down(at).wait_recv()

        middle, last, first = reflected(
            [0, 1, 2],
            [
                window(xt[1], xt[2]),
                window(xt[chunks - 1], up_recv[at]),
                window(down_recv[at], xt[0]),
            ],
        )
        xt[1], xt[2] = middle[:, :band], middle[:, band:]
        xt[chunks - 1] = last[:, :band]
        xt[0] = jnp.where(has_above, first[:, band:], xt[0])
        return carry

    lax.fori_loop(0, rounds, both_levels, 0)

    for i in range(chunks):
        out_ref[i * band : (i + 1) * band, :] = jnp.transpose(xt[i])

    for zz in range(n_z):
        @pl.when(z != zz)
        def _():
            to_z(zz).wait_send()

    for zz in range(n_z):
        to_x(zz, x).wait_send()
        for xx in range(2):
            to_core(zz, xx).wait_send()
    for at in range(rounds):
        @pl.when(has_above)
        def _():
            go_up(at).wait_send()
            half_side(at).wait_send()

        @pl.when(has_below)
        def _():
            go_down(at).wait_send()
            half_down(at).wait_send()


def per_device(n_rows, n_cols, eigvecs, wy_packed, slot_block):
    if n_rows == 2:
        return paired(n_cols, eigvecs, wy_packed, slot_block)
    band = wy_packed.shape[1]
    rows, cols = eigvecs.shape
    levels, per_level = slot_block.shape[1:]
    n_z = n_cols // 4
    rounds = levels // 2
    assert n_cols == levels * per_level and n_z == rounds
    assert wy_packed.shape[0] == 1 and per_level == 2 and rows == 4 * band
    blocks = pltpu.VMEM((rounds, band, band), F32)
    slots = pltpu.VMEM((rounds, cols, band), F32)
    vmem = pl.BlockSpec(memory_space=pltpu.VMEM)
    in_order = pltpu.SemaphoreType.DMA((2, rounds))
    return pl.pallas_call(
        functools.partial(kernel, levels, n_rows, n_z),
        out_shape=jax.ShapeDtypeStruct(eigvecs.shape, F32),
        in_specs=[pl.BlockSpec(memory_space=pltpu.SMEM), vmem, vmem],
        out_specs=vmem,
        scratch_shapes=[
            pltpu.VMEM((n_cols, band, band), F32),
            pltpu.VMEM((rows // band, cols, band), F32),
            pltpu.VMEM((5, 4, band, 2 * band), BF16),
            pltpu.VMEM((rounds, band // 2, band), F32),
            blocks,
            slots,
            slots,
            slots,
            slots,
            pltpu.SemaphoreType.DMA((n_cols,)),
            pltpu.SemaphoreType.DMA((n_cols // 2, 2)),
            pltpu.SemaphoreType.DMA((n_z,)),
            in_order,
            in_order,
            in_order,
            in_order,
        ],
        compiler_params=pltpu.CompilerParams(collective_id=0, has_side_effects=True),
    )(jnp.swapaxes(slot_block, 1, 2), eigvecs, wy_packed)


def solution(mesh):
    placed = (P("rows", "cols"), P(("rows", "cols"), None, None), P("rows", None, None))
    return jax.shard_map(
        functools.partial(per_device, mesh.shape["rows"], mesh.shape["cols"]),
        mesh=mesh, in_specs=placed, out_specs=P("rows", "cols"), check_vma=False,
    )
```

```python
import functools

import jax
import jax.numpy as jnp
from jax import lax
from jax.experimental import pallas as pl
from jax.experimental.pallas import tpu as pltpu
from jax.sharding import PartitionSpec as P

MESH = pl.DeviceIdType.MESH
F32 = jnp.float32
BF16 = jnp.bfloat16
NN = (((1,), (0,)), ((), ()))
NT = (((1,), (1,)), ((), ()))


def split(value):
    high = value.astype(BF16)
    low = (value - high.astype(F32)).astype(BF16)
    return high, low


def product(a, b, dims=NN):
    dot = functools.partial(lax.dot_general, dimension_numbers=dims, preferred_element_type=F32)
    if dims == NN:
        stacked = jnp.concatenate([a[0], a[1]], axis=1)
        return dot(stacked, jnp.concatenate([b[0], b[0]], axis=0)) + dot(a[0], b[1])
    return dot(a[0], b[0]) + (dot(a[0], b[1]) + dot(a[1], b[0]))


def inverses(grams, multiply):
    band = grams[0].shape[0]
    small = 16
    row = lax.broadcasted_iota(jnp.int32, (band, band), 0)
    col = lax.broadcasted_iota(jnp.int32, (band, band), 1)
    zero = jnp.zeros((band, band), F32)
    upper = col > row
    near = row // small == col // small
    stricts = [jnp.where(upper, gram, zero) for gram in grams]

    at = lax.broadcasted_iota(jnp.int32, (small, band), 0)
    lane = lax.broadcasted_iota(jnp.int32, (small, band), 1)
    first = lane // small * small
    on_diagonal = lane - first == at
    none = jnp.zeros((small, band), F32)

    def gathered(value, index):
        return jnp.take_along_axis(value, index, axis=1)

    def side_by_side(value):
        parts = [value[i : i + small] for i in range(0, band, small)]
        return functools.reduce(jnp.add, parts)

    packed = [side_by_side(jnp.where(near, gram, zero)) for gram in grams]
    scales = [
        2.0 / jnp.sum(jnp.where(on_diagonal, p, none), axis=0, keepdims=True) for p in packed
    ]
    scaled = [
        jnp.where(lane - first > at, p, none) * s for p, s in zip(packed, scales)
    ]
    solved = [jnp.where(on_diagonal, 1.0, none) for _ in grams]
    for m in range(small - 1, 0, -1):
        columns = [gathered(s, first + m) for s in scaled]
        solved = [r - a * r[m : m + 1] for r, a in zip(solved, columns)]
    by_row = [gathered(jnp.broadcast_to(s, (small, band)), first + at) for s in scales]
    solved = [r * s for r, s in zip(solved, by_row)]
    found = [
        jnp.where(near, jnp.concatenate([r] * (band // small), axis=0), zero) for r in solved
    ]

    width = small
    while width < band:
        factor = 2 if band // width % 4 else 4
        wide = width * factor
        inside = (row // wide == col // wide) & (row // width != col // width)
        corners = [jnp.where(inside, strict, zero) for strict in stricts]
        powers = [multiply(a, b) for a, b in zip(found, corners)]
        firsts = [multiply(n, a) for n, a in zip(powers, found)]
        found = [a - b for a, b in zip(found, firsts)]
        if factor == 4:
            squares = [multiply(n, n) for n in powers]
            seconds = [multiply(n, a) for n, a in zip(squares, found)]
            found = [a + b for a, b in zip(found, seconds)]
        width = wide
    return found


def fast(a, b):
    return product(split(a), split(b))


def spread(w):
    band = w.shape[0]
    row = lax.broadcasted_iota(jnp.int32, (band, band), 0)
    col = lax.broadcasted_iota(jnp.int32, (band, band), 1)
    upper = col >= row
    zero = jnp.zeros((band, band), F32)
    return jnp.concatenate([jnp.where(upper, w, zero), jnp.where(upper, zero, w)], axis=1)


def own_blocks(sheared):
    v_parts = [split(spread(w)) for w in sheared]
    grams = [product(v, v, NT) for v in v_parts]
    factors = inverses(grams, fast)
    return [product(split(t), v) for t, v in zip(factors, v_parts)]


def paired_kernel(
    levels, n_z, slot_ref, eig_ref, wy_ref, out_ref,
    raw, vz, xin, xt, ops, flags,
    raw_recv, own_send, relay_send, core_recv, core_send, side_sem, local_sem,
):
    band = wy_ref.shape[1]
    chunks = eig_ref.shape[0] // band
    per_level = chunks // 2
    windows = 2 * per_level
    g = lax.axis_index("rows")
    c = lax.axis_index("cols")
    z, x, k = c // 4, (c // 2) % 2, c % 2
    flip_g, flip_x = 1 - 2 * g, 1 - 2 * x
    p1 = {"rows": 1 - g, "cols": c}
    p2 = {"rows": g, "cols": c + 2 * flip_x}
    p3 = {"rows": 1 - g, "cols": c + 2 * flip_x}
    core_partner = {"rows": g, "cols": c + 1 - 2 * k}
    row_partner = {"rows": 1 - g, "cols": c}

    def z_mate(zz):
        return {"rows": g, "cols": c + 4 * (zz - z)}

    own = g * levels + z * 2 + x
    opposite = (1 - g) * levels + z * 2 + 1 - x

    local_v = pltpu.make_async_copy(wy_ref.at[0], raw.at[own], local_sem.at[0])
    local_x = pltpu.make_async_copy(eig_ref, xin.at[g], local_sem.at[1])
    local_v.start()
    local_x.start()

    barrier = pltpu.get_barrier_semaphore()
    for d in range(1, n_z):
        pl.semaphore_signal(
            barrier, inc=1, device_id=z_mate((z + d) % n_z), device_id_type=MESH
        )
    for other in (p1, p2, p3, core_partner):
        pl.semaphore_signal(barrier, inc=1, device_id=other, device_id_type=MESH)

    level_row = lax.broadcasted_iota(jnp.int32, (levels, band), 0)
    tile = jnp.zeros((levels, band), F32)
    for level in range(levels):
        tile = jnp.where(level_row == level, slot_ref[0, 0, level].astype(F32), tile)
    flags[g] = tile
    xt[2 * chunks] = jnp.zeros((eig_ref.shape[1], band), F32)

    def remote(src, dst, send, recv, target):
        return pltpu.make_async_remote_copy(
            src_ref=src, dst_ref=dst, send_sem=send, recv_sem=recv,
            device_id=target, device_id_type=MESH,
        )

    def from_own(at, target):
        return remote(raw.at[own], raw.at[own], own_send.at[at], raw_recv.at[own], target)

    def to_z(zz):
        return from_own(zz, z_mate(zz))

    def relay(q, zz, way, target):
        return remote(raw.at[q], raw.at[q], relay_send.at[zz, way], raw_recv.at[q], target)

    def across(q):
        return remote(vz.at[k, q], vz.at[k, q], core_send.at[q], core_recv.at[q], core_partner)

    def flags_across():
        return remote(flags.at[g], flags.at[g], side_sem.at[0, 0], side_sem.at[1, 0], row_partner)

    def x_across():
        return remote(eig_ref, xin.at[g], side_sem.at[0, 1], side_sem.at[1, 1], row_partner)

    local_v.wait()
    pl.semaphore_wait(barrier, n_z + 3)

    @pl.when(k == 0)
    def _():
        from_own(n_z + 2, p3).start()

    for zz in range(n_z - 1, -1, -1):
        @pl.when(zz != z)
        def _():
            to_z(zz).start()
    from_own(n_z, p1).start()
    from_own(n_z + 1, p2).start()
    flags_across().start()

    def other(i):
        return i + (z <= i).astype(jnp.int32)

    def plane(step):
        zz = jnp.where(step == 0, z, other(step - 1))
        at = zz * 2 + x
        mine = g * levels + at
        across_y = (1 - g) * levels + at
        across_x = g * levels + at + flip_x
        across_both = (1 - g) * levels + at + flip_x
        blocks = [mine, across_y, across_x, across_both]

        @pl.when((step == 0) & (k == 0))
        def _():
            relay(across_both, 0, 0, p1).wait_recv()
            for d in range(n_z - 1, 0, -1):
                far = (z + d) % n_z
                relay(opposite, far, 2, z_mate(far)).start()

        @pl.when((step == 0) & (k == 1))
        def _():
            relay(across_y, 0, 0, p1).wait_recv()
            relay(across_y, z, 2, p2).start()

        @pl.when(step == 0)
        def _():
            for i in range(n_z - 1):
                far = other(i)
                q = g * levels + far * 2 + x
                relay(q, far, 0, p1).wait_recv()
                relay(q, far, 0, p1).start()
                relay(q, far, 1, p2).start()
            x_across().start()

        @pl.when(k == 0)
        def _():
            relay(across_y, 0, 0, p1).wait_recv()

        @pl.when((step > 0) | (k == 1))
        def _():
            relay(across_both, 0, 0, p1).wait_recv()

        relay(across_x, 0, 0, p1).wait_recv()
        sheared = [pltpu.roll(jnp.transpose(raw[q]), 0, 1, stride=1, stride_axis=0) for q in blocks]
        for q, w, zed in zip(blocks, sheared, own_blocks(sheared)):
            vz[k, q, 0] = w
            vz[k, q, 1] = zed[:, :band]
            vz[k, q, 2] = zed[:, band:]
        for q in blocks:
            across(q).start()

        @pl.when((step == 0) & (k == 1))
        def _():
            for i in range(n_z - 1):
                far = other(i)
                q = (1 - g) * levels + far * 2 + x
                relay(q, far, 0, p1).wait_recv()
                relay(q, far, 2, p2).start()


    def ready(level, base):
        for r in range(2):
            q = r * levels + level
            first = flags[r, pl.ds(level, 1), :] < 0.5
            a, b = vz[0, q], vz[1, q]
            for h, w in enumerate((jnp.where(first, a, b), jnp.where(first, b, a))):
                v = split(spread(w[0]))
                zed = split(jnp.concatenate([w[1], w[2]], axis=1))
                at = base + r * per_level + h
                ops[at, 0], ops[at, 1] = zed
                ops[at, 2], ops[at, 3] = v

    def reflected(base, shift):
        pairs = [
            jnp.concatenate([xt[2 * i + shift], xt[2 * i + shift + 1]], axis=1)
            for i in range(windows)
        ]
        halves = [split(pair) for pair in pairs]
        projected = [
            split(product(h, (ops[base + i, 0], ops[base + i, 1]), NT))
            for i, h in enumerate(halves)
        ]
        for i, (pair, y) in enumerate(zip(pairs, projected)):
            new = pair - product(y, (ops[base + i, 2], ops[base + i, 3]))
            xt[2 * i + shift] = new[:, :band]
            if 2 * i + shift + 1 < 2 * chunks:
                xt[2 * i + shift + 1] = new[:, band:]

    def both_levels(at):
        @pl.when(at == 0)
        def _():
            local_x.wait()
            x_across().wait_recv()
            flags_across().wait_recv()
            for r in range(2):
                for i in range(chunks):
                    xt[r * chunks + i] = jnp.transpose(xin[r, i * band : (i + 1) * band, :])

        for i in range(2):
            for r in range(2):
                across(r * levels + 2 * at + i).wait_recv()
        ready(2 * at, 0)
        ready(2 * at + 1, windows)
        reflected(0, 0)
        reflected(windows, 1)

    def turn(step, carry):
        @pl.when(step < n_z)
        def _():
            plane(step)

        @pl.when(step >= 2)
        def _():
            both_levels(step - 2)

        return carry

    lax.fori_loop(0, n_z + 2, turn, 0)

    for i in range(chunks):
        out_ref[i * band : (i + 1) * band, :] = jnp.transpose(xt[g * chunks + i])

    for zz in range(n_z):
        q = own + 2 * (zz - z)

        @pl.when(zz != z)
        def _():
            to_z(zz).wait_send()
            relay(q, zz, 0, p1).wait_send()
            relay(q, zz, 1, p2).wait_send()

        @pl.when((zz != z) | (k == 1))
        def _():
            relay(q, zz, 2, p2).wait_send()

    from_own(n_z, p1).wait_send()
    from_own(n_z + 1, p2).wait_send()

    @pl.when(k == 0)
    def _():
        from_own(n_z + 2, p3).wait_send()

    flags_across().wait_send()
    x_across().wait_send()
    for q in range(2 * levels):
        across(q).wait_send()


def paired(n_cols, eigvecs, wy_packed, slot_block):
    band = wy_packed.shape[1]
    rows, cols = eigvecs.shape
    levels, per_level = slot_block.shape[1:]
    n_z = n_cols // 4
    chunks = rows // band
    assert n_cols == levels * per_level and 2 * n_z == levels
    assert wy_packed.shape[0] == 1 and per_level == 2 and chunks == 2 * per_level
    anywhere = pl.BlockSpec(memory_space=pl.ANY)
    dma = pltpu.SemaphoreType.DMA
    return pl.pallas_call(
        functools.partial(paired_kernel, levels, n_z),
        out_shape=jax.ShapeDtypeStruct(eigvecs.shape, F32),
        in_specs=[pl.BlockSpec(memory_space=pltpu.SMEM), anywhere, anywhere],
        out_specs=pl.BlockSpec(memory_space=pltpu.VMEM),
        scratch_shapes=[
            pltpu.VMEM((2 * levels, band, band), F32),
            pltpu.VMEM((2, 2 * levels, 3, band, band), F32),
            pltpu.VMEM((2, rows, cols), F32),
            pltpu.VMEM((2 * chunks + 1, cols, band), F32),
            pltpu.VMEM((4 * per_level, 4, band, 2 * band), BF16),
            pltpu.VMEM((2, levels, band), F32),
            dma((2 * levels,)),
            dma((n_z + 3,)),
            dma((n_z, 3)),
            dma((2 * levels,)),
            dma((2 * levels,)),
            dma((2, 2)),
            dma((2,)),
        ],
        compiler_params=pltpu.CompilerParams(collective_id=0, has_side_effects=True),
    )(jnp.swapaxes(slot_block, 1, 2), eigvecs, wy_packed)


def kernel(
    levels, n_rows, n_z, slot_ref, eig_ref, wy_ref, out_ref,
    wg, xt, ops, half_send, above, up_send, up_recv, down_send, down_recv,
    recv_sem, send_sem, own_sem, up_sem, down_sem, half_sem, side_sem,
):
    band = wy_ref.shape[1]
    chunks = eig_ref.shape[0] // band
    per_level = chunks // 2
    rounds = levels // 2
    g = lax.axis_index("rows")
    c = lax.axis_index("cols")
    z, x, k = c // 4, (c // 2) % 2, c % 2
    x_partner = z * 4 + (1 - x) * 2 + k
    core_partner = z * 4 + x * 2 + (1 - k)
    z_mates = [((z + d) % n_z) * 4 + x * 2 + k for d in range(1, n_z)]
    has_above = g > 0
    has_below = g < n_rows - 1

    barrier = pltpu.get_barrier_semaphore()
    for other in z_mates + [x_partner, core_partner]:
        pl.semaphore_signal(barrier, inc=1, device_id={"cols": other}, device_id_type=MESH)

    @pl.when(has_above)
    def _():
        pl.semaphore_signal(barrier, inc=1, device_id={"rows": g - 1}, device_id_type=MESH)

    @pl.when(has_below)
    def _():
        pl.semaphore_signal(barrier, inc=1, device_id={"rows": g + 1}, device_id_type=MESH)

    def block_copy(block, target, sem):
        return pltpu.make_async_remote_copy(
            src_ref=wg.at[block],
            dst_ref=wg.at[block],
            send_sem=sem,
            recv_sem=recv_sem.at[block],
            device_id={"cols": target},
            device_id_type=MESH,
        )

    def to_x(zz, xx):
        return block_copy(zz * 4 + xx * 2 + k, x_partner, send_sem.at[zz * 2 + xx, 0])

    def to_core(zz, xx):
        return block_copy(zz * 4 + xx * 2 + k, core_partner, send_sem.at[zz * 2 + xx, 1])

    def to_z(zz):
        return block_copy(c, zz * 4 + x * 2 + k, own_sem.at[zz])

    def relay_z(zz):
        @pl.when(z != zz)
        def _():
            to_x(zz, x).wait_recv()
            to_x(zz, x).start()
            to_core(zz, x).start()

    def relay_x(zz):
        to_core(zz, 1 - x).wait_recv()
        to_core(zz, 1 - x).start()

    def wait_core(zz):
        for xx in range(2):
            block_copy(zz * 4 + xx * 2 + 1 - k, core_partner, send_sem.at[0, 0]).wait_recv()

    def row_copy(src, dst, sem, at, target):
        return pltpu.make_async_remote_copy(
            src_ref=src.at[at],
            dst_ref=dst.at[at],
            send_sem=sem.at[0, at],
            recv_sem=sem.at[1, at],
            device_id={"rows": target},
            device_id_type=MESH,
        )

    def go_up(at):
        return row_copy(up_send, up_recv, up_sem, at, g - 1)

    def go_down(at):
        return row_copy(down_send, down_recv, down_sem, at, g + 1)

    half = band // 2

    def half_down(at):
        return pltpu.make_async_remote_copy(
            src_ref=half_send.at[at],
            dst_ref=above.at[at, pl.ds(k * half, half)],
            send_sem=half_sem.at[0, at],
            recv_sem=half_sem.at[1, at],
            device_id={"rows": g + 1},
            device_id_type=MESH,
        )

    def half_side(at):
        return pltpu.make_async_remote_copy(
            src_ref=above.at[at, pl.ds(k * half, half)],
            dst_ref=above.at[at, pl.ds(k * half, half)],
            send_sem=side_sem.at[0, at],
            recv_sem=side_sem.at[1, at],
            device_id={"cols": core_partner},
            device_id_type=MESH,
        )

    def send_half(at):
        level = 2 * at + 1
        first = slot_ref[0, per_level - 1, level] == 0
        rows = pl.ds(k * half, half)
        half_send[at] = jnp.where(
            first, wg[level * per_level, rows], wg[level * per_level + 1, rows]
        )
        half_down(at).start()

    wg[c] = pltpu.roll(jnp.transpose(wy_ref[0]), 0, 1, stride=1, stride_axis=0)
    pl.semaphore_wait(
        barrier, n_z + 1 + has_above.astype(jnp.int32) + has_below.astype(jnp.int32)
    )
    to_x(z, x).start()
    to_core(z, x).start()
    for far in range(n_z - 1, -1, -1):
        @pl.when((far != z) & ((far < z) | (z < 2)))
        def _():
            to_z(far).start()

    @pl.when(jnp.logical_not(has_above))
    def _():
        above[...] = jnp.zeros_like(above)
        down_recv[...] = jnp.zeros_like(down_recv)

    @pl.when(jnp.logical_not(has_below))
    def _():
        up_recv[...] = jnp.zeros_like(up_recv)

    for i in range(chunks):
        xt[i] = jnp.transpose(eig_ref[i * band : (i + 1) * band, :])

    def chosen(level, h):
        first = slot_ref[0, h, level] == 0
        return jnp.where(first, wg[level * per_level], wg[level * per_level + 1])

    def prepare(sheared, places):
        v_parts = [split(spread(w)) for w in sheared]
        grams = [product(v, v, NT) for v in v_parts]
        factors = inverses(grams, fast)
        for place, v, t in zip(places, v_parts, factors):
            z_parts = split(product(split(t), v))
            ops[place, 0] = z_parts[0]
            ops[place, 1] = z_parts[1]
            ops[place, 2] = v[0]
            ops[place, 3] = v[1]

    def reflected(places, pairs):
        halves = [split(pair) for pair in pairs]
        projected = [
            split(product(x, (ops[p, 0], ops[p, 1]), NT)) for p, x in zip(places, halves)
        ]
        return [
            pair - product(y, (ops[p, 2], ops[p, 3]))
            for p, y, pair in zip(places, projected, pairs)
        ]

    def window(top, bottom):
        return jnp.concatenate([top, bottom], axis=1)

    relay_z(0)

    @pl.when(z >= 2)
    def _():
        for far in range(n_z - 1, 2, -1):
            @pl.when(far > z)
            def _():
                to_z(far).start()

    relay_x(0)
    wait_core(0)

    @pl.when(has_below)
    def _():
        send_half(0)

    relay_z(1)
    prepare([chosen(0, 0), chosen(0, 1)], [3, 4])

    def both_levels(at, carry):
        @pl.when(has_above)
        def _():
            half_down(at).wait_recv()
            half_side(at).start()

        upper_new, lower_new = reflected([3, 4], [window(xt[0], xt[1]), window(xt[2], xt[3])])
        xt[0], xt[1] = upper_new[:, :band], upper_new[:, band:]
        xt[2], xt[3] = lower_new[:, :band], lower_new[:, band:]

        @pl.when(has_above)
        def _():
            up_send[at] = xt[0]
            go_up(at).start()

        @pl.when(has_below)
        def _():
            down_send[at] = xt[chunks - 1]
            go_down(at).start()

        @pl.when(at < rounds - 1)
        def _():
            relay_x(at + 1)
            wait_core(at + 1)

            @pl.when(has_below)
            def _():
                send_half(at + 1)

        @pl.when(at < rounds - 2)
        def _():
            relay_z(at + 2)

        @pl.when(has_above)
        def _():
            half_side(at).wait_recv()

        odd, even = 2 * at + 1, (2 * at + 2) % levels
        prepare(
            [chosen(odd, 0), chosen(odd, 1), above[at], chosen(even, 0), chosen(even, 1)],
            [0, 1, 2, 3, 4],
        )

        @pl.when(has_below)
        def _():
            go_up(at).wait_recv()

        @pl.when(has_above)
        def _():
            go_down(at).wait_recv()

        middle, last, first = reflected(
            [0, 1, 2],
            [
                window(xt[1], xt[2]),
                window(xt[chunks - 1], up_recv[at]),
                window(down_recv[at], xt[0]),
            ],
        )
        xt[1], xt[2] = middle[:, :band], middle[:, band:]
        xt[chunks - 1] = last[:, :band]
        xt[0] = jnp.where(has_above, first[:, band:], xt[0])
        return carry

    lax.fori_loop(0, rounds, both_levels, 0)

    for i in range(chunks):
        out_ref[i * band : (i + 1) * band, :] = jnp.transpose(xt[i])

    for zz in range(n_z):
        @pl.when(z != zz)
        def _():
            to_z(zz).wait_send()

    for zz in range(n_z):
        to_x(zz, x).wait_send()
        for xx in range(2):
            to_core(zz, xx).wait_send()
    for at in range(rounds):
        @pl.when(has_above)
        def _():
            go_up(at).wait_send()
            half_side(at).wait_send()

        @pl.when(has_below)
        def _():
            go_down(at).wait_send()
            half_down(at).wait_send()


def per_device(n_rows, n_cols, eigvecs, wy_packed, slot_block):
    if n_rows == 2:
        return paired(n_cols, eigvecs, wy_packed, slot_block)
    band = wy_packed.shape[1]
    rows, cols = eigvecs.shape
    levels, per_level = slot_block.shape[1:]
    n_z = n_cols // 4
    rounds = levels // 2
    assert n_cols == levels * per_level and n_z == rounds
    assert wy_packed.shape[0] == 1 and per_level == 2 and rows == 4 * band
    blocks = pltpu.VMEM((rounds, band, band), F32)
    slots = pltpu.VMEM((rounds, cols, band), F32)
    vmem = pl.BlockSpec(memory_space=pltpu.VMEM)
    in_order = pltpu.SemaphoreType.DMA((2, rounds))
    return pl.pallas_call(
        functools.partial(kernel, levels, n_rows, n_z),
        out_shape=jax.ShapeDtypeStruct(eigvecs.shape, F32),
        in_specs=[pl.BlockSpec(memory_space=pltpu.SMEM), vmem, vmem],
        out_specs=vmem,
        scratch_shapes=[
            pltpu.VMEM((n_cols, band, band), F32),
            pltpu.VMEM((rows // band, cols, band), F32),
            pltpu.VMEM((5, 4, band, 2 * band), BF16),
            pltpu.VMEM((rounds, band // 2, band), F32),
            blocks,
            slots,
            slots,
            slots,
            slots,
            pltpu.SemaphoreType.DMA((n_cols,)),
            pltpu.SemaphoreType.DMA((n_cols // 2, 2)),
            pltpu.SemaphoreType.DMA((n_z,)),
            in_order,
            in_order,
            in_order,
            in_order,
        ],
        compiler_params=pltpu.CompilerParams(collective_id=0, has_side_effects=True),
    )(jnp.swapaxes(slot_block, 1, 2), eigvecs, wy_packed)


def solution(mesh):
    placed = (P("rows", "cols"), P(("rows", "cols"), None, None), P("rows", None, None))
    return jax.shard_map(
        functools.partial(per_device, mesh.shape["rows"], mesh.shape["cols"]),
        mesh=mesh, in_specs=placed, out_specs=P("rows", "cols"), check_vma=False,
    )
```

```python
import functools

import jax
import jax.numpy as jnp
from jax import lax
from jax.experimental import pallas as pl
from jax.experimental.pallas import tpu as pltpu
from jax.sharding import PartitionSpec as P

MESH = pl.DeviceIdType.MESH
F32 = jnp.float32
BF16 = jnp.bfloat16
NN = (((1,), (0,)), ((), ()))
NT = (((1,), (1,)), ((), ()))


def split(value):
    high = value.astype(BF16)
    low = (value - high.astype(F32)).astype(BF16)
    return high, low


def product(a, b, dims=NN):
    dot = functools.partial(lax.dot_general, dimension_numbers=dims, preferred_element_type=F32)
    if dims == NN:
        stacked = jnp.concatenate([a[0], a[1]], axis=1)
        return dot(stacked, jnp.concatenate([b[0], b[0]], axis=0)) + dot(a[0], b[1])
    return dot(a[0], b[0]) + (dot(a[0], b[1]) + dot(a[1], b[0]))


def inverses(grams, multiply):
    band = grams[0].shape[0]
    small = 16
    row = lax.broadcasted_iota(jnp.int32, (band, band), 0)
    col = lax.broadcasted_iota(jnp.int32, (band, band), 1)
    zero = jnp.zeros((band, band), F32)
    upper = col > row
    near = row // small == col // small
    stricts = [jnp.where(upper, gram, zero) for gram in grams]

    at = lax.broadcasted_iota(jnp.int32, (small, band), 0)
    lane = lax.broadcasted_iota(jnp.int32, (small, band), 1)
    first = lane // small * small
    on_diagonal = lane - first == at
    none = jnp.zeros((small, band), F32)

    def gathered(value, index):
        return jnp.take_along_axis(value, index, axis=1)

    def side_by_side(value):
        parts = [value[i : i + small] for i in range(0, band, small)]
        return functools.reduce(jnp.add, parts)

    packed = [side_by_side(jnp.where(near, gram, zero)) for gram in grams]
    scales = [
        2.0 / jnp.sum(jnp.where(on_diagonal, p, none), axis=0, keepdims=True) for p in packed
    ]
    scaled = [
        jnp.where(lane - first > at, p, none) * s for p, s in zip(packed, scales)
    ]
    solved = [jnp.where(on_diagonal, 1.0, none) for _ in grams]
    for m in range(small - 1, 0, -1):
        columns = [gathered(s, first + m) for s in scaled]
        solved = [r - a * r[m : m + 1] for r, a in zip(solved, columns)]
    by_row = [gathered(jnp.broadcast_to(s, (small, band)), first + at) for s in scales]
    solved = [r * s for r, s in zip(solved, by_row)]
    found = [
        jnp.where(near, jnp.concatenate([r] * (band // small), axis=0), zero) for r in solved
    ]

    width = small
    while width < band:
        factor = 2 if band // width % 4 else 4
        wide = width * factor
        inside = (row // wide == col // wide) & (row // width != col // width)
        corners = [jnp.where(inside, strict, zero) for strict in stricts]
        powers = [multiply(a, b) for a, b in zip(found, corners)]
        firsts = [multiply(n, a) for n, a in zip(powers, found)]
        found = [a - b for a, b in zip(found, firsts)]
        if factor == 4:
            squares = [multiply(n, n) for n in powers]
            seconds = [multiply(n, a) for n, a in zip(squares, found)]
            found = [a + b for a, b in zip(found, seconds)]
        width = wide
    return found


def fast(a, b):
    return product(split(a), split(b))


def spread(w):
    band = w.shape[0]
    row = lax.broadcasted_iota(jnp.int32, (band, band), 0)
    col = lax.broadcasted_iota(jnp.int32, (band, band), 1)
    upper = col >= row
    zero = jnp.zeros((band, band), F32)
    return jnp.concatenate([jnp.where(upper, w, zero), jnp.where(upper, zero, w)], axis=1)


def own_blocks(sheared):
    v_parts = [split(spread(w)) for w in sheared]
    grams = [product(v, v, NT) for v in v_parts]
    factors = inverses(grams, fast)
    return [product(split(t), v) for t, v in zip(factors, v_parts)]


def paired_kernel(
    levels, n_z, slot_ref, eig_ref, wy_ref, out_ref,
    raw, vz, xin, xt, ops, flags,
    raw_recv, own_send, relay_send, core_recv, core_send, side_sem, local_sem,
):
    band = wy_ref.shape[1]
    chunks = eig_ref.shape[0] // band
    per_level = chunks // 2
    windows = 2 * per_level
    g = lax.axis_index("rows")
    c = lax.axis_index("cols")
    z, x, k = c // 4, (c // 2) % 2, c % 2
    flip_g, flip_x = 1 - 2 * g, 1 - 2 * x
    p1 = {"rows": 1 - g, "cols": c}
    p2 = {"rows": g, "cols": c + 2 * flip_x}
    p3 = {"rows": 1 - g, "cols": c + 2 * flip_x}
    core_partner = {"rows": g, "cols": c + 1 - 2 * k}
    row_partner = {"rows": 1 - g, "cols": c}

    side = jnp.where(z < n_z // 2, 1, n_z - 1)

    def near(i):
        return (z + side * (i + 1)) % n_z

    def upward(i):
        return i + (z <= i).astype(jnp.int32)

    def z_mate(zz):
        return {"rows": g, "cols": c + 4 * (zz - z)}

    own = g * levels + z * 2 + x
    opposite = (1 - g) * levels + z * 2 + 1 - x

    local_v = pltpu.make_async_copy(wy_ref.at[0], raw.at[own], local_sem.at[0])
    local_x = pltpu.make_async_copy(eig_ref, xin.at[g], local_sem.at[1])
    local_v.start()
    local_x.start()

    barrier = pltpu.get_barrier_semaphore()
    for d in range(1, n_z):
        pl.semaphore_signal(
            barrier, inc=1, device_id=z_mate((z + d) % n_z), device_id_type=MESH
        )
    for other in (p1, p2, p3, core_partner):
        pl.semaphore_signal(barrier, inc=1, device_id=other, device_id_type=MESH)

    level_row = lax.broadcasted_iota(jnp.int32, (levels, band), 0)
    tile = jnp.zeros((levels, band), F32)
    for level in range(levels):
        tile = jnp.where(level_row == level, slot_ref[0, 0, level].astype(F32), tile)
    flags[g] = tile
    xt[2 * chunks] = jnp.zeros((eig_ref.shape[1], band), F32)

    def remote(src, dst, send, recv, target):
        return pltpu.make_async_remote_copy(
            src_ref=src, dst_ref=dst, send_sem=send, recv_sem=recv,
            device_id=target, device_id_type=MESH,
        )

    def from_own(at, target):
        return remote(raw.at[own], raw.at[own], own_send.at[at], raw_recv.at[own], target)

    def to_z(zz):
        return from_own(zz, z_mate(zz))

    def relay(q, zz, way, target):
        return remote(raw.at[q], raw.at[q], relay_send.at[zz, way], raw_recv.at[q], target)

    def across(q):
        return remote(vz.at[k, q], vz.at[k, q], core_send.at[q], core_recv.at[q], core_partner)

    def flags_across():
        return remote(flags.at[g], flags.at[g], side_sem.at[0, 0], side_sem.at[1, 0], row_partner)

    def x_across():
        return remote(eig_ref, xin.at[g], side_sem.at[0, 1], side_sem.at[1, 1], row_partner)

    local_v.wait()
    pl.semaphore_wait(barrier, n_z + 3)

    @pl.when(k == 0)
    def _():
        from_own(n_z + 2, p3).start()

    for i in range(n_z - 1):
        to_z(near(i)).start()
    from_own(n_z, p1).start()
    from_own(n_z + 1, p2).start()
    flags_across().start()

    def plane(step):
        zz = jnp.where(step == 0, z, upward(step - 1))
        at = zz * 2 + x
        mine = g * levels + at
        across_y = (1 - g) * levels + at
        across_x = g * levels + at + flip_x
        across_both = (1 - g) * levels + at + flip_x
        blocks = [mine, across_y, across_x, across_both]

        @pl.when((step == 0) & (k == 0))
        def _():
            relay(across_both, 0, 0, p1).wait_recv()
            for d in range(n_z - 1, 0, -1):
                far = (z + d) % n_z
                relay(opposite, far, 2, z_mate(far)).start()

        @pl.when((step == 0) & (k == 1))
        def _():
            relay(across_y, 0, 0, p1).wait_recv()
            relay(across_y, z, 2, p2).start()

        @pl.when(step == 0)
        def _():
            for i in range(n_z - 1):
                far = upward(i)
                q = g * levels + far * 2 + x
                relay(q, far, 0, p1).wait_recv()
                relay(q, far, 0, p1).start()
                relay(q, far, 1, p2).start()
            x_across().start()

        @pl.when(k == 0)
        def _():
            relay(across_y, 0, 0, p1).wait_recv()

        @pl.when((step > 0) | (k == 1))
        def _():
            relay(across_both, 0, 0, p1).wait_recv()

        relay(across_x, 0, 0, p1).wait_recv()
        sheared = [pltpu.roll(jnp.transpose(raw[q]), 0, 1, stride=1, stride_axis=0) for q in blocks]
        for q, w, zed in zip(blocks, sheared, own_blocks(sheared)):
            vz[k, q, 0] = w
            vz[k, q, 1] = zed[:, :band]
            vz[k, q, 2] = zed[:, band:]
        for q in blocks:
            across(q).start()

        @pl.when((step == 0) & (k == 1))
        def _():
            for i in range(n_z - 1):
                far = upward(i)
                q = (1 - g) * levels + far * 2 + x
                relay(q, far, 0, p1).wait_recv()
                relay(q, far, 2, p2).start()


    def ready(level, base):
        for r in range(2):
            q = r * levels + level
            first = flags[r, pl.ds(level, 1), :] < 0.5
            a, b = vz[0, q], vz[1, q]
            for h, w in enumerate((jnp.where(first, a, b), jnp.where(first, b, a))):
                v = split(spread(w[0]))
                zed = split(jnp.concatenate([w[1], w[2]], axis=1))
                at = base + r * per_level + h
                ops[at, 0], ops[at, 1] = zed
                ops[at, 2], ops[at, 3] = v

    def reflected(base, shift):
        pairs = [
            jnp.concatenate([xt[2 * i + shift], xt[2 * i + shift + 1]], axis=1)
            for i in range(windows)
        ]
        halves = [split(pair) for pair in pairs]
        projected = [
            split(product(h, (ops[base + i, 0], ops[base + i, 1]), NT))
            for i, h in enumerate(halves)
        ]
        for i, (pair, y) in enumerate(zip(pairs, projected)):
            new = pair - product(y, (ops[base + i, 2], ops[base + i, 3]))
            xt[2 * i + shift] = new[:, :band]
            if 2 * i + shift + 1 < 2 * chunks:
                xt[2 * i + shift + 1] = new[:, band:]

    def both_levels(at):
        @pl.when(at == 0)
        def _():
            local_x.wait()
            x_across().wait_recv()
            flags_across().wait_recv()
            for r in range(2):
                for i in range(chunks):
                    xt[r * chunks + i] = jnp.transpose(xin[r, i * band : (i + 1) * band, :])

        for i in range(2):
            for r in range(2):
                across(r * levels + 2 * at + i).wait_recv()
        ready(2 * at, 0)
        ready(2 * at + 1, windows)
        reflected(0, 0)
        reflected(windows, 1)

    def turn(step, carry):
        @pl.when(step < n_z)
        def _():
            plane(step)

        @pl.when(step >= 3)
        def _():
            both_levels(step - 3)

        return carry

    lax.fori_loop(0, n_z + 3, turn, 0)

    for i in range(chunks):
        out_ref[i * band : (i + 1) * band, :] = jnp.transpose(xt[g * chunks + i])

    for zz in range(n_z):
        q = own + 2 * (zz - z)

        @pl.when(zz != z)
        def _():
            to_z(zz).wait_send()
            relay(q, zz, 0, p1).wait_send()
            relay(q, zz, 1, p2).wait_send()

        @pl.when((zz != z) | (k == 1))
        def _():
            relay(q, zz, 2, p2).wait_send()

    from_own(n_z, p1).wait_send()
    from_own(n_z + 1, p2).wait_send()

    @pl.when(k == 0)
    def _():
        from_own(n_z + 2, p3).wait_send()

    flags_across().wait_send()
    x_across().wait_send()
    for q in range(2 * levels):
        across(q).wait_send()


def paired(n_cols, eigvecs, wy_packed, slot_block):
    band = wy_packed.shape[1]
    rows, cols = eigvecs.shape
    levels, per_level = slot_block.shape[1:]
    n_z = n_cols // 4
    chunks = rows // band
    assert n_cols == levels * per_level and 2 * n_z == levels
    assert wy_packed.shape[0] == 1 and per_level == 2 and chunks == 2 * per_level
    anywhere = pl.BlockSpec(memory_space=pl.ANY)
    dma = pltpu.SemaphoreType.DMA
    return pl.pallas_call(
        functools.partial(paired_kernel, levels, n_z),
        out_shape=jax.ShapeDtypeStruct(eigvecs.shape, F32),
        in_specs=[pl.BlockSpec(memory_space=pltpu.SMEM), anywhere, anywhere],
        out_specs=pl.BlockSpec(memory_space=pltpu.VMEM),
        scratch_shapes=[
            pltpu.VMEM((2 * levels, band, band), F32),
            pltpu.VMEM((2, 2 * levels, 3, band, band), F32),
            pltpu.VMEM((2, rows, cols), F32),
            pltpu.VMEM((2 * chunks + 1, cols, band), F32),
            pltpu.VMEM((4 * per_level, 4, band, 2 * band), BF16),
            pltpu.VMEM((2, levels, band), F32),
            dma((2 * levels,)),
            dma((n_z + 3,)),
            dma((n_z, 3)),
            dma((2 * levels,)),
            dma((2 * levels,)),
            dma((2, 2)),
            dma((2,)),
        ],
        compiler_params=pltpu.CompilerParams(collective_id=0, has_side_effects=True),
    )(jnp.swapaxes(slot_block, 1, 2), eigvecs, wy_packed)


def kernel(
    levels, n_rows, n_z, slot_ref, eig_ref, wy_ref, out_ref,
    wg, xt, ops, half_send, above, up_send, up_recv, down_send, down_recv,
    recv_sem, send_sem, own_sem, up_sem, down_sem, half_sem, side_sem,
):
    band = wy_ref.shape[1]
    chunks = eig_ref.shape[0] // band
    per_level = chunks // 2
    rounds = levels // 2
    g = lax.axis_index("rows")
    c = lax.axis_index("cols")
    z, x, k = c // 4, (c // 2) % 2, c % 2
    x_partner = z * 4 + (1 - x) * 2 + k
    core_partner = z * 4 + x * 2 + (1 - k)
    z_mates = [((z + d) % n_z) * 4 + x * 2 + k for d in range(1, n_z)]
    has_above = g > 0
    has_below = g < n_rows - 1

    barrier = pltpu.get_barrier_semaphore()
    for other in z_mates + [x_partner, core_partner]:
        pl.semaphore_signal(barrier, inc=1, device_id={"cols": other}, device_id_type=MESH)

    @pl.when(has_above)
    def _():
        pl.semaphore_signal(barrier, inc=1, device_id={"rows": g - 1}, device_id_type=MESH)

    @pl.when(has_below)
    def _():
        pl.semaphore_signal(barrier, inc=1, device_id={"rows": g + 1}, device_id_type=MESH)

    def block_copy(block, target, sem):
        return pltpu.make_async_remote_copy(
            src_ref=wg.at[block],
            dst_ref=wg.at[block],
            send_sem=sem,
            recv_sem=recv_sem.at[block],
            device_id={"cols": target},
            device_id_type=MESH,
        )

    def to_x(zz, xx):
        return block_copy(zz * 4 + xx * 2 + k, x_partner, send_sem.at[zz * 2 + xx, 0])

    def to_core(zz, xx):
        return block_copy(zz * 4 + xx * 2 + k, core_partner, send_sem.at[zz * 2 + xx, 1])

    def to_z(zz):
        return block_copy(c, zz * 4 + x * 2 + k, own_sem.at[zz])

    def relay_z(zz):
        @pl.when(z != zz)
        def _():
            to_x(zz, x).wait_recv()
            to_x(zz, x).start()
            to_core(zz, x).start()

    def relay_x(zz):
        to_core(zz, 1 - x).wait_recv()
        to_core(zz, 1 - x).start()

    def wait_core(zz):
        for xx in range(2):
            block_copy(zz * 4 + xx * 2 + 1 - k, core_partner, send_sem.at[0, 0]).wait_recv()

    def row_copy(src, dst, sem, at, target):
        return pltpu.make_async_remote_copy(
            src_ref=src.at[at],
            dst_ref=dst.at[at],
            send_sem=sem.at[0, at],
            recv_sem=sem.at[1, at],
            device_id={"rows": target},
            device_id_type=MESH,
        )

    def go_up(at):
        return row_copy(up_send, up_recv, up_sem, at, g - 1)

    def go_down(at):
        return row_copy(down_send, down_recv, down_sem, at, g + 1)

    half = band // 2

    def half_down(at):
        return pltpu.make_async_remote_copy(
            src_ref=half_send.at[at],
            dst_ref=above.at[at, pl.ds(k * half, half)],
            send_sem=half_sem.at[0, at],
            recv_sem=half_sem.at[1, at],
            device_id={"rows": g + 1},
            device_id_type=MESH,
        )

    def half_side(at):
        return pltpu.make_async_remote_copy(
            src_ref=above.at[at, pl.ds(k * half, half)],
            dst_ref=above.at[at, pl.ds(k * half, half)],
            send_sem=side_sem.at[0, at],
            recv_sem=side_sem.at[1, at],
            device_id={"cols": core_partner},
            device_id_type=MESH,
        )

    def send_half(at):
        level = 2 * at + 1
        first = slot_ref[0, per_level - 1, level] == 0
        rows = pl.ds(k * half, half)
        half_send[at] = jnp.where(
            first, wg[level * per_level, rows], wg[level * per_level + 1, rows]
        )
        half_down(at).start()

    wg[c] = pltpu.roll(jnp.transpose(wy_ref[0]), 0, 1, stride=1, stride_axis=0)
    pl.semaphore_wait(
        barrier, n_z + 1 + has_above.astype(jnp.int32) + has_below.astype(jnp.int32)
    )
    to_x(z, x).start()
    to_core(z, x).start()
    for far in range(n_z - 1, -1, -1):
        @pl.when((far != z) & ((far < z) | (z < 2)))
        def _():
            to_z(far).start()

    @pl.when(jnp.logical_not(has_above))
    def _():
        above[...] = jnp.zeros_like(above)
        down_recv[...] = jnp.zeros_like(down_recv)

    @pl.when(jnp.logical_not(has_below))
    def _():
        up_recv[...] = jnp.zeros_like(up_recv)

    for i in range(chunks):
        xt[i] = jnp.transpose(eig_ref[i * band : (i + 1) * band, :])

    def chosen(level, h):
        first = slot_ref[0, h, level] == 0
        return jnp.where(first, wg[level * per_level], wg[level * per_level + 1])

    def prepare(sheared, places):
        v_parts = [split(spread(w)) for w in sheared]
        grams = [product(v, v, NT) for v in v_parts]
        factors = inverses(grams, fast)
        for place, v, t in zip(places, v_parts, factors):
            z_parts = split(product(split(t), v))
            ops[place, 0] = z_parts[0]
            ops[place, 1] = z_parts[1]
            ops[place, 2] = v[0]
            ops[place, 3] = v[1]

    def reflected(places, pairs):
        halves = [split(pair) for pair in pairs]
        projected = [
            split(product(x, (ops[p, 0], ops[p, 1]), NT)) for p, x in zip(places, halves)
        ]
        return [
            pair - product(y, (ops[p, 2], ops[p, 3]))
            for p, y, pair in zip(places, projected, pairs)
        ]

    def window(top, bottom):
        return jnp.concatenate([top, bottom], axis=1)

    relay_z(0)

    @pl.when(z >= 2)
    def _():
        for far in range(n_z - 1, 2, -1):
            @pl.when(far > z)
            def _():
                to_z(far).start()

    relay_x(0)
    wait_core(0)

    @pl.when(has_below)
    def _():
        send_half(0)

    relay_z(1)
    prepare([chosen(0, 0), chosen(0, 1)], [3, 4])

    def both_levels(at, carry):
        @pl.when(has_above)
        def _():
            half_down(at).wait_recv()
            half_side(at).start()

        upper_new, lower_new = reflected([3, 4], [window(xt[0], xt[1]), window(xt[2], xt[3])])
        xt[0], xt[1] = upper_new[:, :band], upper_new[:, band:]
        xt[2], xt[3] = lower_new[:, :band], lower_new[:, band:]

        @pl.when(has_above)
        def _():
            up_send[at] = xt[0]
            go_up(at).start()

        @pl.when(has_below)
        def _():
            down_send[at] = xt[chunks - 1]
            go_down(at).start()

        @pl.when(at < rounds - 1)
        def _():
            relay_x(at + 1)
            wait_core(at + 1)

            @pl.when(has_below)
            def _():
                send_half(at + 1)

        @pl.when(at < rounds - 2)
        def _():
            relay_z(at + 2)

        @pl.when(has_above)
        def _():
            half_side(at).wait_recv()

        odd, even = 2 * at + 1, (2 * at + 2) % levels
        prepare(
            [chosen(odd, 0), chosen(odd, 1), above[at], chosen(even, 0), chosen(even, 1)],
            [0, 1, 2, 3, 4],
        )

        @pl.when(has_below)
        def _():
            go_up(at).wait_recv()

        @pl.when(has_above)
        def _():
            go_down(at).wait_recv()

        middle, last, first = reflected(
            [0, 1, 2],
            [
                window(xt[1], xt[2]),
                window(xt[chunks - 1], up_recv[at]),
                window(down_recv[at], xt[0]),
            ],
        )
        xt[1], xt[2] = middle[:, :band], middle[:, band:]
        xt[chunks - 1] = last[:, :band]
        xt[0] = jnp.where(has_above, first[:, band:], xt[0])
        return carry

    lax.fori_loop(0, rounds, both_levels, 0)

    for i in range(chunks):
        out_ref[i * band : (i + 1) * band, :] = jnp.transpose(xt[i])

    for zz in range(n_z):
        @pl.when(z != zz)
        def _():
            to_z(zz).wait_send()

    for zz in range(n_z):
        to_x(zz, x).wait_send()
        for xx in range(2):
            to_core(zz, xx).wait_send()
    for at in range(rounds):
        @pl.when(has_above)
        def _():
            go_up(at).wait_send()
            half_side(at).wait_send()

        @pl.when(has_below)
        def _():
            go_down(at).wait_send()
            half_down(at).wait_send()


def per_device(n_rows, n_cols, eigvecs, wy_packed, slot_block):
    if n_rows == 2:
        return paired(n_cols, eigvecs, wy_packed, slot_block)
    band = wy_packed.shape[1]
    rows, cols = eigvecs.shape
    levels, per_level = slot_block.shape[1:]
    n_z = n_cols // 4
    rounds = levels // 2
    assert n_cols == levels * per_level and n_z == rounds
    assert wy_packed.shape[0] == 1 and per_level == 2 and rows == 4 * band
    blocks = pltpu.VMEM((rounds, band, band), F32)
    slots = pltpu.VMEM((rounds, cols, band), F32)
    vmem = pl.BlockSpec(memory_space=pltpu.VMEM)
    in_order = pltpu.SemaphoreType.DMA((2, rounds))
    return pl.pallas_call(
        functools.partial(kernel, levels, n_rows, n_z),
        out_shape=jax.ShapeDtypeStruct(eigvecs.shape, F32),
        in_specs=[pl.BlockSpec(memory_space=pltpu.SMEM), vmem, vmem],
        out_specs=vmem,
        scratch_shapes=[
            pltpu.VMEM((n_cols, band, band), F32),
            pltpu.VMEM((rows // band, cols, band), F32),
            pltpu.VMEM((5, 4, band, 2 * band), BF16),
            pltpu.VMEM((rounds, band // 2, band), F32),
            blocks,
            slots,
            slots,
            slots,
            slots,
            pltpu.SemaphoreType.DMA((n_cols,)),
            pltpu.SemaphoreType.DMA((n_cols // 2, 2)),
            pltpu.SemaphoreType.DMA((n_z,)),
            in_order,
            in_order,
            in_order,
            in_order,
        ],
        compiler_params=pltpu.CompilerParams(collective_id=0, has_side_effects=True),
    )(jnp.swapaxes(slot_block, 1, 2), eigvecs, wy_packed)


def solution(mesh):
    placed = (P("rows", "cols"), P(("rows", "cols"), None, None), P("rows", None, None))
    return jax.shard_map(
        functools.partial(per_device, mesh.shape["rows"], mesh.shape["cols"]),
        mesh=mesh, in_specs=placed, out_specs=P("rows", "cols"), check_vma=False,
    )
```

```python
import functools

import jax
import jax.numpy as jnp
from jax import lax
from jax.experimental import pallas as pl
from jax.experimental.pallas import tpu as pltpu
from jax.sharding import PartitionSpec as P

MESH = pl.DeviceIdType.MESH
F32 = jnp.float32
BF16 = jnp.bfloat16
NN = (((1,), (0,)), ((), ()))
NT = (((1,), (1,)), ((), ()))


def split(value):
    high = value.astype(BF16)
    low = (value - high.astype(F32)).astype(BF16)
    return high, low


def product(a, b, dims=NN):
    dot = functools.partial(lax.dot_general, dimension_numbers=dims, preferred_element_type=F32)
    if dims == NN:
        stacked = jnp.concatenate([a[0], a[1]], axis=1)
        cols = b[0].shape[1]
        if cols == a[0].shape[1]:
            upper = jnp.concatenate([b[0], b[1]], axis=1)
            lower = jnp.concatenate([b[0], jnp.zeros_like(b[1])], axis=1)
            both = dot(stacked, jnp.concatenate([upper, lower], axis=0))
            return both[:, :cols] + both[:, cols:]
        return dot(stacked, jnp.concatenate([b[0], b[0]], axis=0)) + dot(a[0], b[1])
    both = dot(a[0], jnp.concatenate([b[0], b[1]], axis=0))
    rows = b[0].shape[0]
    return both[:, :rows] + (both[:, rows:] + dot(a[1], b[0]))


def inverses(grams, multiply):
    band = grams[0].shape[0]
    small = 16
    row = lax.broadcasted_iota(jnp.int32, (band, band), 0)
    col = lax.broadcasted_iota(jnp.int32, (band, band), 1)
    zero = jnp.zeros((band, band), F32)
    upper = col > row
    near = row // small == col // small
    stricts = [jnp.where(upper, gram, zero) for gram in grams]

    at = lax.broadcasted_iota(jnp.int32, (small, band), 0)
    lane = lax.broadcasted_iota(jnp.int32, (small, band), 1)
    first = lane // small * small
    on_diagonal = lane - first == at
    none = jnp.zeros((small, band), F32)

    def gathered(value, index):
        return jnp.take_along_axis(value, index, axis=1)

    def side_by_side(value):
        parts = [value[i : i + small] for i in range(0, band, small)]
        return functools.reduce(jnp.add, parts)

    packed = [side_by_side(jnp.where(near, gram, zero)) for gram in grams]
    scales = [
        2.0 / jnp.sum(jnp.where(on_diagonal, p, none), axis=0, keepdims=True) for p in packed
    ]
    scaled = [
        jnp.where(lane - first > at, p, none) * s for p, s in zip(packed, scales)
    ]
    solved = [jnp.where(on_diagonal, 1.0, none) for _ in grams]
    for m in range(small - 1, 0, -1):
        columns = [gathered(s, first + m) for s in scaled]
        solved = [r - a * r[m : m + 1] for r, a in zip(solved, columns)]
    by_row = [gathered(jnp.broadcast_to(s, (small, band)), first + at) for s in scales]
    solved = [r * s for r, s in zip(solved, by_row)]
    found = [
        jnp.where(near, jnp.concatenate([r] * (band // small), axis=0), zero) for r in solved
    ]

    width = small
    while width < band:
        factor = 2 if band // width % 4 else 4
        wide = width * factor
        inside = (row // wide == col // wide) & (row // width != col // width)
        corners = [jnp.where(inside, strict, zero) for strict in stricts]
        powers = [multiply(a, b) for a, b in zip(found, corners)]
        firsts = [multiply(n, a) for n, a in zip(powers, found)]
        found = [a - b for a, b in zip(found, firsts)]
        if factor == 4:
            squares = [multiply(n, n) for n in powers]
            seconds = [multiply(n, a) for n, a in zip(squares, found)]
            found = [a + b for a, b in zip(found, seconds)]
        width = wide
    return found


def fast(a, b):
    return product(split(a), split(b))


def spread(w):
    band = w.shape[0]
    row = lax.broadcasted_iota(jnp.int32, (band, band), 0)
    col = lax.broadcasted_iota(jnp.int32, (band, band), 1)
    upper = col >= row
    zero = jnp.zeros((band, band), F32)
    return jnp.concatenate([jnp.where(upper, w, zero), jnp.where(upper, zero, w)], axis=1)


def own_blocks(sheared):
    v_parts = [split(spread(w)) for w in sheared]
    grams = [product(v, v, NT) for v in v_parts]
    factors = inverses(grams, fast)
    return [product(split(t), v) for t, v in zip(factors, v_parts)]


def paired_kernel(
    levels, n_z, slot_ref, eig_ref, wy_ref, out_ref,
    raw, vz, xin, xt, ops, flags,
    raw_recv, own_send, relay_send, core_recv, core_send, side_sem, local_sem,
):
    band = wy_ref.shape[1]
    chunks = eig_ref.shape[0] // band
    per_level = chunks // 2
    windows = 2 * per_level
    g = lax.axis_index("rows")
    c = lax.axis_index("cols")
    z, x, k = c // 4, (c // 2) % 2, c % 2
    flip_g, flip_x = 1 - 2 * g, 1 - 2 * x
    p1 = {"rows": 1 - g, "cols": c}
    p2 = {"rows": g, "cols": c + 2 * flip_x}
    p3 = {"rows": 1 - g, "cols": c + 2 * flip_x}
    core_partner = {"rows": g, "cols": c + 1 - 2 * k}
    row_partner = {"rows": 1 - g, "cols": c}

    side = jnp.where(z < n_z // 2, 1, n_z - 1)

    def near(i):
        return (z + side * (i + 1)) % n_z

    def upward(i):
        return i + (z <= i).astype(jnp.int32)

    def z_mate(zz):
        return {"rows": g, "cols": c + 4 * (zz - z)}

    own = g * levels + z * 2 + x
    opposite = (1 - g) * levels + z * 2 + 1 - x

    local_v = pltpu.make_async_copy(wy_ref.at[0], raw.at[own], local_sem.at[0])
    local_x = pltpu.make_async_copy(eig_ref, xin.at[g], local_sem.at[1])
    local_v.start()
    local_x.start()

    barrier = pltpu.get_barrier_semaphore()
    for d in range(1, n_z):
        pl.semaphore_signal(
            barrier, inc=1, device_id=z_mate((z + d) % n_z), device_id_type=MESH
        )
    for other in (p1, p2, p3, core_partner):
        pl.semaphore_signal(barrier, inc=1, device_id=other, device_id_type=MESH)

    level_row = lax.broadcasted_iota(jnp.int32, (levels, band), 0)
    tile = jnp.zeros((levels, band), F32)
    for level in range(levels):
        tile = jnp.where(level_row == level, slot_ref[0, 0, level].astype(F32), tile)
    flags[g] = tile
    xt[2 * chunks] = jnp.zeros((eig_ref.shape[1], band), F32)

    def remote(src, dst, send, recv, target):
        return pltpu.make_async_remote_copy(
            src_ref=src, dst_ref=dst, send_sem=send, recv_sem=recv,
            device_id=target, device_id_type=MESH,
        )

    def from_own(at, target):
        return remote(raw.at[own], raw.at[own], own_send.at[at], raw_recv.at[own], target)

    def to_z(zz):
        return from_own(zz, z_mate(zz))

    def relay(q, zz, way, target):
        return remote(raw.at[q], raw.at[q], relay_send.at[zz, way], raw_recv.at[q], target)

    def across(q):
        return remote(vz.at[k, q], vz.at[k, q], core_send.at[q], core_recv.at[q], core_partner)

    def flags_across():
        return remote(flags.at[g], flags.at[g], side_sem.at[0, 0], side_sem.at[1, 0], row_partner)

    def x_across():
        return remote(eig_ref, xin.at[g], side_sem.at[0, 1], side_sem.at[1, 1], row_partner)

    local_v.wait()
    pl.semaphore_wait(barrier, n_z + 3)

    @pl.when(k == 0)
    def _():
        from_own(n_z + 2, p3).start()

    for i in range(n_z - 1):
        to_z(near(i)).start()
    from_own(n_z, p1).start()
    from_own(n_z + 1, p2).start()
    flags_across().start()

    def plane(step):
        zz = jnp.where(step == 0, z, upward(step - 1))
        at = zz * 2 + x
        mine = g * levels + at
        across_y = (1 - g) * levels + at
        across_x = g * levels + at + flip_x
        across_both = (1 - g) * levels + at + flip_x
        blocks = [mine, across_y, across_x, across_both]

        @pl.when((step == 0) & (k == 0))
        def _():
            relay(across_both, 0, 0, p1).wait_recv()
            for d in range(n_z - 1, 0, -1):
                far = (z + d) % n_z
                relay(opposite, far, 2, z_mate(far)).start()

        @pl.when((step == 0) & (k == 1))
        def _():
            relay(across_y, 0, 0, p1).wait_recv()
            relay(across_y, z, 2, p2).start()

        @pl.when(step == 0)
        def _():
            for i in range(n_z - 1):
                far = upward(i)
                q = g * levels + far * 2 + x
                relay(q, far, 0, p1).wait_recv()
                relay(q, far, 0, p1).start()
                relay(q, far, 1, p2).start()
            x_across().start()

        @pl.when(k == 0)
        def _():
            relay(across_y, 0, 0, p1).wait_recv()

        @pl.when((step > 0) | (k == 1))
        def _():
            relay(across_both, 0, 0, p1).wait_recv()

        relay(across_x, 0, 0, p1).wait_recv()
        sheared = [pltpu.roll(jnp.transpose(raw[q]), 0, 1, stride=1, stride_axis=0) for q in blocks]
        for q, w, zed in zip(blocks, sheared, own_blocks(sheared)):
            vz[k, q, 0] = w
            vz[k, q, 1] = zed[:, :band]
            vz[k, q, 2] = zed[:, band:]
        for q in blocks:
            across(q).start()

        @pl.when((step == 0) & (k == 1))
        def _():
            for i in range(n_z - 1):
                far = upward(i)
                q = (1 - g) * levels + far * 2 + x
                relay(q, far, 0, p1).wait_recv()
                relay(q, far, 2, p2).start()


    def ready(level, base):
        for r in range(2):
            q = r * levels + level
            first = flags[r, pl.ds(level, 1), :] < 0.5
            a, b = vz[0, q], vz[1, q]
            for h, w in enumerate((jnp.where(first, a, b), jnp.where(first, b, a))):
                v = split(spread(w[0]))
                zed = split(jnp.concatenate([w[1], w[2]], axis=1))
                at = base + r * per_level + h
                ops[at, 0], ops[at, 1] = zed
                ops[at, 2], ops[at, 3] = v

    def reflected(base, shift):
        pairs = [
            jnp.concatenate([xt[2 * i + shift], xt[2 * i + shift + 1]], axis=1)
            for i in range(windows)
        ]
        halves = [split(pair) for pair in pairs]
        projected = [
            split(product(h, (ops[base + i, 0], ops[base + i, 1]), NT))
            for i, h in enumerate(halves)
        ]
        for i, (pair, y) in enumerate(zip(pairs, projected)):
            new = pair - product(y, (ops[base + i, 2], ops[base + i, 3]))
            xt[2 * i + shift] = new[:, :band]
            if 2 * i + shift + 1 < 2 * chunks:
                xt[2 * i + shift + 1] = new[:, band:]

    def both_levels(at):
        @pl.when(at == 0)
        def _():
            local_x.wait()
            x_across().wait_recv()
            flags_across().wait_recv()
            for r in range(2):
                for i in range(chunks):
                    xt[r * chunks + i] = jnp.transpose(xin[r, i * band : (i + 1) * band, :])

        for i in range(2):
            for r in range(2):
                across(r * levels + 2 * at + i).wait_recv()
        ready(2 * at, 0)
        ready(2 * at + 1, windows)
        reflected(0, 0)
        reflected(windows, 1)

    def turn(step, carry):
        @pl.when(step < n_z)
        def _():
            plane(step)

        @pl.when(step >= 3)
        def _():
            both_levels(step - 3)

        return carry

    lax.fori_loop(0, n_z + 3, turn, 0)

    for i in range(chunks):
        out_ref[i * band : (i + 1) * band, :] = jnp.transpose(xt[g * chunks + i])

    for zz in range(n_z):
        q = own + 2 * (zz - z)

        @pl.when(zz != z)
        def _():
            to_z(zz).wait_send()
            relay(q, zz, 0, p1).wait_send()
            relay(q, zz, 1, p2).wait_send()

        @pl.when((zz != z) | (k == 1))
        def _():
            relay(q, zz, 2, p2).wait_send()

    from_own(n_z, p1).wait_send()
    from_own(n_z + 1, p2).wait_send()

    @pl.when(k == 0)
    def _():
        from_own(n_z + 2, p3).wait_send()

    flags_across().wait_send()
    x_across().wait_send()
    for q in range(2 * levels):
        across(q).wait_send()


def paired(n_cols, eigvecs, wy_packed, slot_block):
    band = wy_packed.shape[1]
    rows, cols = eigvecs.shape
    levels, per_level = slot_block.shape[1:]
    n_z = n_cols // 4
    chunks = rows // band
    assert n_cols == levels * per_level and 2 * n_z == levels
    assert wy_packed.shape[0] == 1 and per_level == 2 and chunks == 2 * per_level
    anywhere = pl.BlockSpec(memory_space=pl.ANY)
    dma = pltpu.SemaphoreType.DMA
    return pl.pallas_call(
        functools.partial(paired_kernel, levels, n_z),
        out_shape=jax.ShapeDtypeStruct(eigvecs.shape, F32),
        in_specs=[pl.BlockSpec(memory_space=pltpu.SMEM), anywhere, anywhere],
        out_specs=pl.BlockSpec(memory_space=pltpu.VMEM),
        scratch_shapes=[
            pltpu.VMEM((2 * levels, band, band), F32),
            pltpu.VMEM((2, 2 * levels, 3, band, band), F32),
            pltpu.VMEM((2, rows, cols), F32),
            pltpu.VMEM((2 * chunks + 1, cols, band), F32),
            pltpu.VMEM((4 * per_level, 4, band, 2 * band), BF16),
            pltpu.VMEM((2, levels, band), F32),
            dma((2 * levels,)),
            dma((n_z + 3,)),
            dma((n_z, 3)),
            dma((2 * levels,)),
            dma((2 * levels,)),
            dma((2, 2)),
            dma((2,)),
        ],
        compiler_params=pltpu.CompilerParams(collective_id=0, has_side_effects=True),
    )(jnp.swapaxes(slot_block, 1, 2), eigvecs, wy_packed)


def kernel(
    levels, n_rows, n_z, slot_ref, eig_ref, wy_ref, out_ref,
    wg, xt, ops, half_send, above, up_send, up_recv, down_send, down_recv,
    recv_sem, send_sem, own_sem, up_sem, down_sem, half_sem, side_sem,
):
    band = wy_ref.shape[1]
    chunks = eig_ref.shape[0] // band
    per_level = chunks // 2
    rounds = levels // 2
    g = lax.axis_index("rows")
    c = lax.axis_index("cols")
    z, x, k = c // 4, (c // 2) % 2, c % 2
    x_partner = z * 4 + (1 - x) * 2 + k
    core_partner = z * 4 + x * 2 + (1 - k)
    z_mates = [((z + d) % n_z) * 4 + x * 2 + k for d in range(1, n_z)]
    has_above = g > 0
    has_below = g < n_rows - 1

    barrier = pltpu.get_barrier_semaphore()
    for other in z_mates + [x_partner, core_partner]:
        pl.semaphore_signal(barrier, inc=1, device_id={"cols": other}, device_id_type=MESH)

    @pl.when(has_above)
    def _():
        pl.semaphore_signal(barrier, inc=1, device_id={"rows": g - 1}, device_id_type=MESH)

    @pl.when(has_below)
    def _():
        pl.semaphore_signal(barrier, inc=1, device_id={"rows": g + 1}, device_id_type=MESH)

    def block_copy(block, target, sem):
        return pltpu.make_async_remote_copy(
            src_ref=wg.at[block],
            dst_ref=wg.at[block],
            send_sem=sem,
            recv_sem=recv_sem.at[block],
            device_id={"cols": target},
            device_id_type=MESH,
        )

    def to_x(zz, xx):
        return block_copy(zz * 4 + xx * 2 + k, x_partner, send_sem.at[zz * 2 + xx, 0])

    def to_core(zz, xx):
        return block_copy(zz * 4 + xx * 2 + k, core_partner, send_sem.at[zz * 2 + xx, 1])

    def to_z(zz):
        return block_copy(c, zz * 4 + x * 2 + k, own_sem.at[zz])

    def relay_z(zz):
        @pl.when(z != zz)
        def _():
            to_x(zz, x).wait_recv()
            to_x(zz, x).start()
            to_core(zz, x).start()

    def relay_x(zz):
        to_core(zz, 1 - x).wait_recv()
        to_core(zz, 1 - x).start()

    def wait_core(zz):
        for xx in range(2):
            block_copy(zz * 4 + xx * 2 + 1 - k, core_partner, send_sem.at[0, 0]).wait_recv()

    def row_copy(src, dst, sem, at, target):
        return pltpu.make_async_remote_copy(
            src_ref=src.at[at],
            dst_ref=dst.at[at],
            send_sem=sem.at[0, at],
            recv_sem=sem.at[1, at],
            device_id={"rows": target},
            device_id_type=MESH,
        )

    def go_up(at):
        return row_copy(up_send, up_recv, up_sem, at, g - 1)

    def go_down(at):
        return row_copy(down_send, down_recv, down_sem, at, g + 1)

    half = band // 2

    def half_down(at):
        return pltpu.make_async_remote_copy(
            src_ref=half_send.at[at],
            dst_ref=above.at[at, pl.ds(k * half, half)],
            send_sem=half_sem.at[0, at],
            recv_sem=half_sem.at[1, at],
            device_id={"rows": g + 1},
            device_id_type=MESH,
        )

    def half_side(at):
        return pltpu.make_async_remote_copy(
            src_ref=above.at[at, pl.ds(k * half, half)],
            dst_ref=above.at[at, pl.ds(k * half, half)],
            send_sem=side_sem.at[0, at],
            recv_sem=side_sem.at[1, at],
            device_id={"cols": core_partner},
            device_id_type=MESH,
        )

    def send_half(at):
        level = 2 * at + 1
        first = slot_ref[0, per_level - 1, level] == 0
        rows = pl.ds(k * half, half)
        half_send[at] = jnp.where(
            first, wg[level * per_level, rows], wg[level * per_level + 1, rows]
        )
        half_down(at).start()

    wg[c] = pltpu.roll(jnp.transpose(wy_ref[0]), 0, 1, stride=1, stride_axis=0)
    pl.semaphore_wait(
        barrier, n_z + 1 + has_above.astype(jnp.int32) + has_below.astype(jnp.int32)
    )
    to_x(z, x).start()
    to_core(z, x).start()
    for far in range(n_z - 1, -1, -1):
        @pl.when((far != z) & ((far < z) | (z < 2)))
        def _():
            to_z(far).start()

    @pl.when(jnp.logical_not(has_above))
    def _():
        above[...] = jnp.zeros_like(above)
        down_recv[...] = jnp.zeros_like(down_recv)

    @pl.when(jnp.logical_not(has_below))
    def _():
        up_recv[...] = jnp.zeros_like(up_recv)

    for i in range(chunks):
        xt[i] = jnp.transpose(eig_ref[i * band : (i + 1) * band, :])

    def chosen(level, h):
        first = slot_ref[0, h, level] == 0
        return jnp.where(first, wg[level * per_level], wg[level * per_level + 1])

    def prepare(sheared, places):
        v_parts = [split(spread(w)) for w in sheared]
        grams = [product(v, v, NT) for v in v_parts]
        factors = inverses(grams, fast)
        for place, v, t in zip(places, v_parts, factors):
            z_parts = split(product(split(t), v))
            ops[place, 0] = z_parts[0]
            ops[place, 1] = z_parts[1]
            ops[place, 2] = v[0]
            ops[place, 3] = v[1]

    def reflected(places, pairs):
        halves = [split(pair) for pair in pairs]
        projected = [
            split(product(x, (ops[p, 0], ops[p, 1]), NT)) for p, x in zip(places, halves)
        ]
        return [
            pair - product(y, (ops[p, 2], ops[p, 3]))
            for p, y, pair in zip(places, projected, pairs)
        ]

    def window(top, bottom):
        return jnp.concatenate([top, bottom], axis=1)

    relay_z(0)

    @pl.when(z >= 2)
    def _():
        for far in range(n_z - 1, 2, -1):
            @pl.when(far > z)
            def _():
                to_z(far).start()

    relay_x(0)
    wait_core(0)

    @pl.when(has_below)
    def _():
        send_half(0)

    relay_z(1)
    prepare([chosen(0, 0), chosen(0, 1)], [3, 4])

    def both_levels(at, carry):
        @pl.when(has_above)
        def _():
            half_down(at).wait_recv()
            half_side(at).start()

        upper_new, lower_new = reflected([3, 4], [window(xt[0], xt[1]), window(xt[2], xt[3])])
        xt[0], xt[1] = upper_new[:, :band], upper_new[:, band:]
        xt[2], xt[3] = lower_new[:, :band], lower_new[:, band:]

        @pl.when(has_above)
        def _():
            up_send[at] = xt[0]
            go_up(at).start()

        @pl.when(has_below)
        def _():
            down_send[at] = xt[chunks - 1]
            go_down(at).start()

        @pl.when(at < rounds - 1)
        def _():
            relay_x(at + 1)
            wait_core(at + 1)

            @pl.when(has_below)
            def _():
                send_half(at + 1)

        @pl.when(at < rounds - 2)
        def _():
            relay_z(at + 2)

        @pl.when(has_above)
        def _():
            half_side(at).wait_recv()

        odd, even = 2 * at + 1, (2 * at + 2) % levels
        prepare(
            [chosen(odd, 0), chosen(odd, 1), above[at], chosen(even, 0), chosen(even, 1)],
            [0, 1, 2, 3, 4],
        )

        @pl.when(has_below)
        def _():
            go_up(at).wait_recv()

        @pl.when(has_above)
        def _():
            go_down(at).wait_recv()

        middle, last, first = reflected(
            [0, 1, 2],
            [
                window(xt[1], xt[2]),
                window(xt[chunks - 1], up_recv[at]),
                window(down_recv[at], xt[0]),
            ],
        )
        xt[1], xt[2] = middle[:, :band], middle[:, band:]
        xt[chunks - 1] = last[:, :band]
        xt[0] = jnp.where(has_above, first[:, band:], xt[0])
        return carry

    lax.fori_loop(0, rounds, both_levels, 0)

    for i in range(chunks):
        out_ref[i * band : (i + 1) * band, :] = jnp.transpose(xt[i])

    for zz in range(n_z):
        @pl.when(z != zz)
        def _():
            to_z(zz).wait_send()

    for zz in range(n_z):
        to_x(zz, x).wait_send()
        for xx in range(2):
            to_core(zz, xx).wait_send()
    for at in range(rounds):
        @pl.when(has_above)
        def _():
            go_up(at).wait_send()
            half_side(at).wait_send()

        @pl.when(has_below)
        def _():
            go_down(at).wait_send()
            half_down(at).wait_send()


def per_device(n_rows, n_cols, eigvecs, wy_packed, slot_block):
    if n_rows == 2:
        return paired(n_cols, eigvecs, wy_packed, slot_block)
    band = wy_packed.shape[1]
    rows, cols = eigvecs.shape
    levels, per_level = slot_block.shape[1:]
    n_z = n_cols // 4
    rounds = levels // 2
    assert n_cols == levels * per_level and n_z == rounds
    assert wy_packed.shape[0] == 1 and per_level == 2 and rows == 4 * band
    blocks = pltpu.VMEM((rounds, band, band), F32)
    slots = pltpu.VMEM((rounds, cols, band), F32)
    vmem = pl.BlockSpec(memory_space=pltpu.VMEM)
    in_order = pltpu.SemaphoreType.DMA((2, rounds))
    return pl.pallas_call(
        functools.partial(kernel, levels, n_rows, n_z),
        out_shape=jax.ShapeDtypeStruct(eigvecs.shape, F32),
        in_specs=[pl.BlockSpec(memory_space=pltpu.SMEM), vmem, vmem],
        out_specs=vmem,
        scratch_shapes=[
            pltpu.VMEM((n_cols, band, band), F32),
            pltpu.VMEM((rows // band, cols, band), F32),
            pltpu.VMEM((5, 4, band, 2 * band), BF16),
            pltpu.VMEM((rounds, band // 2, band), F32),
            blocks,
            slots,
            slots,
            slots,
            slots,
            pltpu.SemaphoreType.DMA((n_cols,)),
            pltpu.SemaphoreType.DMA((n_cols // 2, 2)),
            pltpu.SemaphoreType.DMA((n_z,)),
            in_order,
            in_order,
            in_order,
            in_order,
        ],
        compiler_params=pltpu.CompilerParams(collective_id=0, has_side_effects=True),
    )(jnp.swapaxes(slot_block, 1, 2), eigvecs, wy_packed)


def solution(mesh):
    placed = (P("rows", "cols"), P(("rows", "cols"), None, None), P("rows", None, None))
    return jax.shard_map(
        functools.partial(per_device, mesh.shape["rows"], mesh.shape["cols"]),
        mesh=mesh, in_specs=placed, out_specs=P("rows", "cols"), check_vma=False,
    )
```

```python
import functools

import jax
import jax.numpy as jnp
from jax import lax
from jax.experimental import pallas as pl
from jax.experimental.pallas import tpu as pltpu
from jax.sharding import PartitionSpec as P

MESH = pl.DeviceIdType.MESH
F32 = jnp.float32
BF16 = jnp.bfloat16
NN = (((1,), (0,)), ((), ()))
NT = (((1,), (1,)), ((), ()))


def split(value):
    high = value.astype(BF16)
    low = (value - high.astype(F32)).astype(BF16)
    return high, low


def product(a, b, dims=NN):
    dot = functools.partial(lax.dot_general, dimension_numbers=dims, preferred_element_type=F32)
    if dims == NN:
        stacked = jnp.concatenate([a[0], a[1]], axis=1)
        cols = b[0].shape[1]
        if cols == a[0].shape[1]:
            upper = jnp.concatenate([b[0], b[1]], axis=1)
            lower = jnp.concatenate([b[0], jnp.zeros_like(b[1])], axis=1)
            both = dot(stacked, jnp.concatenate([upper, lower], axis=0))
            return both[:, :cols] + both[:, cols:]
        return dot(stacked, jnp.concatenate([b[0], b[0]], axis=0)) + dot(a[0], b[1])
    both = dot(a[0], jnp.concatenate([b[0], b[1]], axis=0))
    rows = b[0].shape[0]
    return both[:, :rows] + (both[:, rows:] + dot(a[1], b[0]))


def inverses(grams, multiply):
    band = grams[0].shape[0]
    small = 16
    row = lax.broadcasted_iota(jnp.int32, (band, band), 0)
    col = lax.broadcasted_iota(jnp.int32, (band, band), 1)
    zero = jnp.zeros((band, band), F32)
    upper = col > row
    near = row // small == col // small
    stricts = [jnp.where(upper, gram, zero) for gram in grams]

    at = lax.broadcasted_iota(jnp.int32, (small, band), 0)
    lane = lax.broadcasted_iota(jnp.int32, (small, band), 1)
    first = lane // small * small
    on_diagonal = lane - first == at
    none = jnp.zeros((small, band), F32)

    def gathered(value, index):
        return jnp.take_along_axis(value, index, axis=1)

    def side_by_side(value):
        parts = [value[i : i + small] for i in range(0, band, small)]
        return functools.reduce(jnp.add, parts)

    packed = [side_by_side(jnp.where(near, gram, zero)) for gram in grams]
    scales = [
        2.0 / jnp.sum(jnp.where(on_diagonal, p, none), axis=0, keepdims=True) for p in packed
    ]
    scaled = [
        jnp.where(lane - first > at, p, none) * s for p, s in zip(packed, scales)
    ]
    solved = [jnp.where(on_diagonal, 1.0, none) for _ in grams]
    for m in range(small - 1, 0, -1):
        columns = [gathered(s, first + m) for s in scaled]
        solved = [r - a * r[m : m + 1] for r, a in zip(solved, columns)]
    by_row = [gathered(jnp.broadcast_to(s, (small, band)), first + at) for s in scales]
    solved = [r * s for r, s in zip(solved, by_row)]
    found = [
        jnp.where(near, jnp.concatenate([r] * (band // small), axis=0), zero) for r in solved
    ]

    width = small
    while width < band:
        factor = 2 if band // width % 4 else 4
        wide = width * factor
        inside = (row // wide == col // wide) & (row // width != col // width)
        corners = [jnp.where(inside, strict, zero) for strict in stricts]
        powers = [multiply(a, b) for a, b in zip(found, corners)]
        firsts = [multiply(n, a) for n, a in zip(powers, found)]
        found = [a - b for a, b in zip(found, firsts)]
        if factor == 4:
            squares = [multiply(n, n) for n in powers]
            seconds = [multiply(n, a) for n, a in zip(squares, found)]
            found = [a + b for a, b in zip(found, seconds)]
        width = wide
    return found


def fast(a, b):
    return product(split(a), split(b))


def spread(w):
    band = w.shape[0]
    row = lax.broadcasted_iota(jnp.int32, (band, band), 0)
    col = lax.broadcasted_iota(jnp.int32, (band, band), 1)
    upper = col >= row
    zero = jnp.zeros((band, band), F32)
    return jnp.concatenate([jnp.where(upper, w, zero), jnp.where(upper, zero, w)], axis=1)


def own_blocks(sheared):
    v_parts = [split(spread(w)) for w in sheared]
    grams = [product(v, v, NT) for v in v_parts]
    factors = inverses(grams, fast)
    return [product(split(t), v) for t, v in zip(factors, v_parts)]


def paired_kernel(
    levels, n_z, slot_ref, eig_ref, wy_ref, out_ref,
    raw, vz, xin, xt, ops, flags,
    raw_recv, own_send, relay_send, core_recv, core_send, side_sem, local_sem,
):
    band = wy_ref.shape[1]
    chunks = eig_ref.shape[0] // band
    per_level = chunks // 2
    windows = 2 * per_level
    g = lax.axis_index("rows")
    c = lax.axis_index("cols")
    z, x, k = c // 4, (c // 2) % 2, c % 2
    flip_g, flip_x = 1 - 2 * g, 1 - 2 * x
    p1 = {"rows": 1 - g, "cols": c}
    p2 = {"rows": g, "cols": c + 2 * flip_x}
    p3 = {"rows": 1 - g, "cols": c + 2 * flip_x}
    core_partner = {"rows": g, "cols": c + 1 - 2 * k}
    row_partner = {"rows": 1 - g, "cols": c}

    side = jnp.where(z < n_z // 2, 1, n_z - 1)

    def near(i):
        return (z + side * (i + 1)) % n_z

    def upward(i):
        return i + (z <= i).astype(jnp.int32)

    def z_mate(zz):
        return {"rows": g, "cols": c + 4 * (zz - z)}

    own = g * levels + z * 2 + x
    opposite = (1 - g) * levels + z * 2 + 1 - x

    local_v = pltpu.make_async_copy(wy_ref.at[0], raw.at[own], local_sem.at[0])
    local_x = pltpu.make_async_copy(eig_ref, xin.at[g], local_sem.at[1])
    local_v.start()
    local_x.start()

    barrier = pltpu.get_barrier_semaphore()
    for d in range(1, n_z):
        pl.semaphore_signal(
            barrier, inc=1, device_id=z_mate((z + d) % n_z), device_id_type=MESH
        )
    for other in (p1, p2, p3, core_partner):
        pl.semaphore_signal(barrier, inc=1, device_id=other, device_id_type=MESH)

    level_row = lax.broadcasted_iota(jnp.int32, (levels, band), 0)
    tile = jnp.zeros((levels, band), F32)
    for level in range(levels):
        tile = jnp.where(level_row == level, slot_ref[0, 0, level].astype(F32), tile)
    flags[g] = tile
    xt[2 * chunks] = jnp.zeros((eig_ref.shape[1], band), F32)

    def remote(src, dst, send, recv, target):
        return pltpu.make_async_remote_copy(
            src_ref=src, dst_ref=dst, send_sem=send, recv_sem=recv,
            device_id=target, device_id_type=MESH,
        )

    def from_own(at, target):
        return remote(raw.at[own], raw.at[own], own_send.at[at], raw_recv.at[own], target)

    def to_z(zz):
        return from_own(zz, z_mate(zz))

    def relay(q, zz, way, target):
        return remote(raw.at[q], raw.at[q], relay_send.at[zz, way], raw_recv.at[q], target)

    def across(q):
        return remote(vz.at[k, q], vz.at[k, q], core_send.at[q], core_recv.at[q], core_partner)

    def flags_across():
        return remote(flags.at[g], flags.at[g], side_sem.at[0, 0], side_sem.at[1, 0], row_partner)

    def x_across():
        return remote(eig_ref, xin.at[g], side_sem.at[0, 1], side_sem.at[1, 1], row_partner)

    local_v.wait()
    pl.semaphore_wait(barrier, n_z + 3)

    @pl.when(k == 0)
    def _():
        from_own(n_z + 2, p3).start()

    for i in range(n_z - 1):
        to_z(near(i)).start()
    from_own(n_z, p1).start()
    from_own(n_z + 1, p2).start()
    flags_across().start()

    def factor(blocks):
        sheared = [pltpu.roll(jnp.transpose(raw[q]), 0, 1, stride=1, stride_axis=0) for q in blocks]
        for q, w, zed in zip(blocks, sheared, own_blocks(sheared)):
            vz[k, q, 0] = w
            vz[k, q, 1] = zed[:, :band]
            vz[k, q, 2] = zed[:, band:]
        for q in blocks:
            across(q).start()

    def plane(step):
        zz = jnp.where(step == 0, z, upward(step - 1))
        at = zz * 2 + x
        mine = g * levels + at
        across_y = (1 - g) * levels + at
        across_x = g * levels + at + flip_x
        across_both = (1 - g) * levels + at + flip_x
        blocks = [mine, across_y, across_x, across_both]

        @pl.when((step == 0) & (k == 0))
        def _():
            relay(across_both, 0, 0, p1).wait_recv()
            for d in range(n_z - 1, 0, -1):
                far = (z + d) % n_z
                relay(opposite, far, 2, z_mate(far)).start()

        @pl.when((step == 0) & (k == 1))
        def _():
            relay(across_y, 0, 0, p1).wait_recv()
            relay(across_y, z, 2, p2).start()

        @pl.when(step == 0)
        def _():
            for i in range(n_z - 1):
                far = upward(i)
                q = g * levels + far * 2 + x
                relay(q, far, 0, p1).wait_recv()
                relay(q, far, 0, p1).start()
                relay(q, far, 1, p2).start()
            x_across().start()

        @pl.when(k == 0)
        def _():
            relay(across_y, 0, 0, p1).wait_recv()

        @pl.when((step > 0) | (k == 1))
        def _():
            relay(across_both, 0, 0, p1).wait_recv()

        relay(across_x, 0, 0, p1).wait_recv()

        @pl.when((step == 0) & (k == 1))
        def _():
            for i in range(n_z - 1):
                far = upward(i)
                q = (1 - g) * levels + far * 2 + x
                relay(q, far, 0, p1).wait_recv()
                relay(q, far, 2, p2).start()

        return blocks


    def ready(level, base):
        for r in range(2):
            q = r * levels + level
            first = flags[r, pl.ds(level, 1), :] < 0.5
            a, b = vz[0, q], vz[1, q]
            for h, w in enumerate((jnp.where(first, a, b), jnp.where(first, b, a))):
                v = split(spread(w[0]))
                zed = split(jnp.concatenate([w[1], w[2]], axis=1))
                at = base + r * per_level + h
                ops[at, 0], ops[at, 1] = zed
                ops[at, 2], ops[at, 3] = v

    def reflected(base, shift):
        pairs = [
            jnp.concatenate([xt[2 * i + shift], xt[2 * i + shift + 1]], axis=1)
            for i in range(windows)
        ]
        halves = [split(pair) for pair in pairs]
        projected = [
            split(product(h, (ops[base + i, 0], ops[base + i, 1]), NT))
            for i, h in enumerate(halves)
        ]
        for i, (pair, y) in enumerate(zip(pairs, projected)):
            new = pair - product(y, (ops[base + i, 2], ops[base + i, 3]))
            xt[2 * i + shift] = new[:, :band]
            if 2 * i + shift + 1 < 2 * chunks:
                xt[2 * i + shift + 1] = new[:, band:]

    def both_levels(at):
        @pl.when(at == 0)
        def _():
            local_x.wait()
            x_across().wait_recv()
            flags_across().wait_recv()
            for r in range(2):
                for i in range(chunks):
                    xt[r * chunks + i] = jnp.transpose(xin[r, i * band : (i + 1) * band, :])

        for i in range(2):
            for r in range(2):
                across(r * levels + 2 * at + i).wait_recv()
        ready(2 * at, 0)
        ready(2 * at + 1, windows)
        reflected(0, 0)
        reflected(windows, 1)

    def turn(step, carry):
        @pl.when(step < n_z - 2)
        def _():
            factor(plane(step))

        @pl.when(step == n_z - 2)
        def _():
            factor(plane(n_z - 2) + plane(n_z - 1))

        @pl.when(step >= n_z - 2)
        def _():
            both_levels(step - (n_z - 2))

        return carry

    lax.fori_loop(0, 2 * n_z - 2, turn, 0)

    for i in range(chunks):
        out_ref[i * band : (i + 1) * band, :] = jnp.transpose(xt[g * chunks + i])

    for zz in range(n_z):
        q = own + 2 * (zz - z)

        @pl.when(zz != z)
        def _():
            to_z(zz).wait_send()
            relay(q, zz, 0, p1).wait_send()
            relay(q, zz, 1, p2).wait_send()

        @pl.when((zz != z) | (k == 1))
        def _():
            relay(q, zz, 2, p2).wait_send()

    from_own(n_z, p1).wait_send()
    from_own(n_z + 1, p2).wait_send()

    @pl.when(k == 0)
    def _():
        from_own(n_z + 2, p3).wait_send()

    flags_across().wait_send()
    x_across().wait_send()
    for q in range(2 * levels):
        across(q).wait_send()


def paired(n_cols, eigvecs, wy_packed, slot_block):
    band = wy_packed.shape[1]
    rows, cols = eigvecs.shape
    levels, per_level = slot_block.shape[1:]
    n_z = n_cols // 4
    chunks = rows // band
    assert n_cols == levels * per_level and 2 * n_z == levels
    assert wy_packed.shape[0] == 1 and per_level == 2 and chunks == 2 * per_level
    anywhere = pl.BlockSpec(memory_space=pl.ANY)
    dma = pltpu.SemaphoreType.DMA
    return pl.pallas_call(
        functools.partial(paired_kernel, levels, n_z),
        out_shape=jax.ShapeDtypeStruct(eigvecs.shape, F32),
        in_specs=[pl.BlockSpec(memory_space=pltpu.SMEM), anywhere, anywhere],
        out_specs=pl.BlockSpec(memory_space=pltpu.VMEM),
        scratch_shapes=[
            pltpu.VMEM((2 * levels, band, band), F32),
            pltpu.VMEM((2, 2 * levels, 3, band, band), F32),
            pltpu.VMEM((2, rows, cols), F32),
            pltpu.VMEM((2 * chunks + 1, cols, band), F32),
            pltpu.VMEM((4 * per_level, 4, band, 2 * band), BF16),
            pltpu.VMEM((2, levels, band), F32),
            dma((2 * levels,)),
            dma((n_z + 3,)),
            dma((n_z, 3)),
            dma((2 * levels,)),
            dma((2 * levels,)),
            dma((2, 2)),
            dma((2,)),
        ],
        compiler_params=pltpu.CompilerParams(collective_id=0, has_side_effects=True),
    )(jnp.swapaxes(slot_block, 1, 2), eigvecs, wy_packed)


def kernel(
    levels, n_rows, n_z, slot_ref, eig_ref, wy_ref, out_ref,
    wg, xt, ops, half_send, above, up_send, up_recv, down_send, down_recv,
    recv_sem, send_sem, own_sem, up_sem, down_sem, half_sem, side_sem,
):
    band = wy_ref.shape[1]
    chunks = eig_ref.shape[0] // band
    per_level = chunks // 2
    rounds = levels // 2
    g = lax.axis_index("rows")
    c = lax.axis_index("cols")
    z, x, k = c // 4, (c // 2) % 2, c % 2
    x_partner = z * 4 + (1 - x) * 2 + k
    core_partner = z * 4 + x * 2 + (1 - k)
    z_mates = [((z + d) % n_z) * 4 + x * 2 + k for d in range(1, n_z)]
    has_above = g > 0
    has_below = g < n_rows - 1

    barrier = pltpu.get_barrier_semaphore()
    for other in z_mates + [x_partner, core_partner]:
        pl.semaphore_signal(barrier, inc=1, device_id={"cols": other}, device_id_type=MESH)

    @pl.when(has_above)
    def _():
        pl.semaphore_signal(barrier, inc=1, device_id={"rows": g - 1}, device_id_type=MESH)

    @pl.when(has_below)
    def _():
        pl.semaphore_signal(barrier, inc=1, device_id={"rows": g + 1}, device_id_type=MESH)

    def block_copy(block, target, sem):
        return pltpu.make_async_remote_copy(
            src_ref=wg.at[block],
            dst_ref=wg.at[block],
            send_sem=sem,
            recv_sem=recv_sem.at[block],
            device_id={"cols": target},
            device_id_type=MESH,
        )

    def to_x(zz, xx):
        return block_copy(zz * 4 + xx * 2 + k, x_partner, send_sem.at[zz * 2 + xx, 0])

    def to_core(zz, xx):
        return block_copy(zz * 4 + xx * 2 + k, core_partner, send_sem.at[zz * 2 + xx, 1])

    def to_z(zz):
        return block_copy(c, zz * 4 + x * 2 + k, own_sem.at[zz])

    def relay_z(zz):
        @pl.when(z != zz)
        def _():
            to_x(zz, x).wait_recv()
            to_x(zz, x).start()
            to_core(zz, x).start()

    def relay_x(zz):
        to_core(zz, 1 - x).wait_recv()
        to_core(zz, 1 - x).start()

    def wait_core(zz):
        for xx in range(2):
            block_copy(zz * 4 + xx * 2 + 1 - k, core_partner, send_sem.at[0, 0]).wait_recv()

    def row_copy(src, dst, sem, at, target):
        return pltpu.make_async_remote_copy(
            src_ref=src.at[at],
            dst_ref=dst.at[at],
            send_sem=sem.at[0, at],
            recv_sem=sem.at[1, at],
            device_id={"rows": target},
            device_id_type=MESH,
        )

    def go_up(at):
        return row_copy(up_send, up_recv, up_sem, at, g - 1)

    def go_down(at):
        return row_copy(down_send, down_recv, down_sem, at, g + 1)

    half = band // 2

    def half_down(at):
        return pltpu.make_async_remote_copy(
            src_ref=half_send.at[at],
            dst_ref=above.at[at, pl.ds(k * half, half)],
            send_sem=half_sem.at[0, at],
            recv_sem=half_sem.at[1, at],
            device_id={"rows": g + 1},
            device_id_type=MESH,
        )

    def half_side(at):
        return pltpu.make_async_remote_copy(
            src_ref=above.at[at, pl.ds(k * half, half)],
            dst_ref=above.at[at, pl.ds(k * half, half)],
            send_sem=side_sem.at[0, at],
            recv_sem=side_sem.at[1, at],
            device_id={"cols": core_partner},
            device_id_type=MESH,
        )

    def send_half(at):
        level = 2 * at + 1
        first = slot_ref[0, per_level - 1, level] == 0
        rows = pl.ds(k * half, half)
        half_send[at] = jnp.where(
            first, wg[level * per_level, rows], wg[level * per_level + 1, rows]
        )
        half_down(at).start()

    wg[c] = pltpu.roll(jnp.transpose(wy_ref[0]), 0, 1, stride=1, stride_axis=0)
    pl.semaphore_wait(
        barrier, n_z + 1 + has_above.astype(jnp.int32) + has_below.astype(jnp.int32)
    )
    to_x(z, x).start()
    to_core(z, x).start()
    for far in range(n_z - 1, -1, -1):
        @pl.when((far != z) & ((far < z) | (z < 2)))
        def _():
            to_z(far).start()

    @pl.when(jnp.logical_not(has_above))
    def _():
        above[...] = jnp.zeros_like(above)
        down_recv[...] = jnp.zeros_like(down_recv)

    @pl.when(jnp.logical_not(has_below))
    def _():
        up_recv[...] = jnp.zeros_like(up_recv)

    for i in range(chunks):
        xt[i] = jnp.transpose(eig_ref[i * band : (i + 1) * band, :])

    def chosen(level, h):
        first = slot_ref[0, h, level] == 0
        return jnp.where(first, wg[level * per_level], wg[level * per_level + 1])

    def prepare(sheared, places):
        v_parts = [split(spread(w)) for w in sheared]
        grams = [product(v, v, NT) for v in v_parts]
        factors = inverses(grams, fast)
        for place, v, t in zip(places, v_parts, factors):
            z_parts = split(product(split(t), v))
            ops[place, 0] = z_parts[0]
            ops[place, 1] = z_parts[1]
            ops[place, 2] = v[0]
            ops[place, 3] = v[1]

    def reflected(places, pairs):
        halves = [split(pair) for pair in pairs]
        projected = [
            split(product(x, (ops[p, 0], ops[p, 1]), NT)) for p, x in zip(places, halves)
        ]
        return [
            pair - product(y, (ops[p, 2], ops[p, 3]))
            for p, y, pair in zip(places, projected, pairs)
        ]

    def window(top, bottom):
        return jnp.concatenate([top, bottom], axis=1)

    relay_z(0)

    @pl.when(z >= 2)
    def _():
        for far in range(n_z - 1, 2, -1):
            @pl.when(far > z)
            def _():
                to_z(far).start()

    relay_x(0)
    wait_core(0)

    @pl.when(has_below)
    def _():
        send_half(0)

    relay_z(1)
    prepare([chosen(0, 0), chosen(0, 1)], [3, 4])

    def both_levels(at, carry):
        @pl.when(has_above)
        def _():
            half_down(at).wait_recv()
            half_side(at).start()

        upper_new, lower_new = reflected([3, 4], [window(xt[0], xt[1]), window(xt[2], xt[3])])
        xt[0], xt[1] = upper_new[:, :band], upper_new[:, band:]
        xt[2], xt[3] = lower_new[:, :band], lower_new[:, band:]

        @pl.when(has_above)
        def _():
            up_send[at] = xt[0]
            go_up(at).start()

        @pl.when(has_below)
        def _():
            down_send[at] = xt[chunks - 1]
            go_down(at).start()

        @pl.when(at < rounds - 1)
        def _():
            relay_x(at + 1)
            wait_core(at + 1)

            @pl.when(has_below)
            def _():
                send_half(at + 1)

        @pl.when(at < rounds - 2)
        def _():
            relay_z(at + 2)

        @pl.when(has_above)
        def _():
            half_side(at).wait_recv()

        odd, even = 2 * at + 1, (2 * at + 2) % levels
        prepare(
            [chosen(odd, 0), chosen(odd, 1), above[at], chosen(even, 0), chosen(even, 1)],
            [0, 1, 2, 3, 4],
        )

        @pl.when(has_below)
        def _():
            go_up(at).wait_recv()

        @pl.when(has_above)
        def _():
            go_down(at).wait_recv()

        middle, last, first = reflected(
            [0, 1, 2],
            [
                window(xt[1], xt[2]),
                window(xt[chunks - 1], up_recv[at]),
                window(down_recv[at], xt[0]),
            ],
        )
        xt[1], xt[2] = middle[:, :band], middle[:, band:]
        xt[chunks - 1] = last[:, :band]
        xt[0] = jnp.where(has_above, first[:, band:], xt[0])
        return carry

    lax.fori_loop(0, rounds, both_levels, 0)

    for i in range(chunks):
        out_ref[i * band : (i + 1) * band, :] = jnp.transpose(xt[i])

    for zz in range(n_z):
        @pl.when(z != zz)
        def _():
            to_z(zz).wait_send()

    for zz in range(n_z):
        to_x(zz, x).wait_send()
        for xx in range(2):
            to_core(zz, xx).wait_send()
    for at in range(rounds):
        @pl.when(has_above)
        def _():
            go_up(at).wait_send()
            half_side(at).wait_send()

        @pl.when(has_below)
        def _():
            go_down(at).wait_send()
            half_down(at).wait_send()


def per_device(n_rows, n_cols, eigvecs, wy_packed, slot_block):
    if n_rows == 2:
        return paired(n_cols, eigvecs, wy_packed, slot_block)
    band = wy_packed.shape[1]
    rows, cols = eigvecs.shape
    levels, per_level = slot_block.shape[1:]
    n_z = n_cols // 4
    rounds = levels // 2
    assert n_cols == levels * per_level and n_z == rounds
    assert wy_packed.shape[0] == 1 and per_level == 2 and rows == 4 * band
    blocks = pltpu.VMEM((rounds, band, band), F32)
    slots = pltpu.VMEM((rounds, cols, band), F32)
    vmem = pl.BlockSpec(memory_space=pltpu.VMEM)
    in_order = pltpu.SemaphoreType.DMA((2, rounds))
    return pl.pallas_call(
        functools.partial(kernel, levels, n_rows, n_z),
        out_shape=jax.ShapeDtypeStruct(eigvecs.shape, F32),
        in_specs=[pl.BlockSpec(memory_space=pltpu.SMEM), vmem, vmem],
        out_specs=vmem,
        scratch_shapes=[
            pltpu.VMEM((n_cols, band, band), F32),
            pltpu.VMEM((rows // band, cols, band), F32),
            pltpu.VMEM((5, 4, band, 2 * band), BF16),
            pltpu.VMEM((rounds, band // 2, band), F32),
            blocks,
            slots,
            slots,
            slots,
            slots,
            pltpu.SemaphoreType.DMA((n_cols,)),
            pltpu.SemaphoreType.DMA((n_cols // 2, 2)),
            pltpu.SemaphoreType.DMA((n_z,)),
            in_order,
            in_order,
            in_order,
            in_order,
        ],
        compiler_params=pltpu.CompilerParams(collective_id=0, has_side_effects=True),
    )(jnp.swapaxes(slot_block, 1, 2), eigvecs, wy_packed)


def solution(mesh):
    placed = (P("rows", "cols"), P(("rows", "cols"), None, None), P("rows", None, None))
    return jax.shard_map(
        functools.partial(per_device, mesh.shape["rows"], mesh.shape["cols"]),
        mesh=mesh, in_specs=placed, out_specs=P("rows", "cols"), check_vma=False,
    )
```

```python
import functools

import jax
import jax.numpy as jnp
from jax import lax
from jax.experimental import pallas as pl
from jax.experimental.pallas import tpu as pltpu
from jax.sharding import PartitionSpec as P

MESH = pl.DeviceIdType.MESH
F32 = jnp.float32
BF16 = jnp.bfloat16
NN = (((1,), (0,)), ((), ()))
NT = (((1,), (1,)), ((), ()))


def split(value):
    high = value.astype(BF16)
    low = (value - high.astype(F32)).astype(BF16)
    return high, low


def product(a, b, dims=NN):
    dot = functools.partial(lax.dot_general, dimension_numbers=dims, preferred_element_type=F32)
    if dims == NN:
        stacked = jnp.concatenate([a[0], a[1]], axis=1)
        cols = b[0].shape[1]
        if cols == a[0].shape[1]:
            upper = jnp.concatenate([b[0], b[1]], axis=1)
            lower = jnp.concatenate([b[0], jnp.zeros_like(b[1])], axis=1)
            both = dot(stacked, jnp.concatenate([upper, lower], axis=0))
            return both[:, :cols] + both[:, cols:]
        return dot(stacked, jnp.concatenate([b[0], b[0]], axis=0)) + dot(a[0], b[1])
    both = dot(a[0], jnp.concatenate([b[0], b[1]], axis=0))
    rows = b[0].shape[0]
    return both[:, :rows] + (both[:, rows:] + dot(a[1], b[0]))


def inverses(grams, multiply):
    band = grams[0].shape[0]
    small = 16
    row = lax.broadcasted_iota(jnp.int32, (band, band), 0)
    col = lax.broadcasted_iota(jnp.int32, (band, band), 1)
    zero = jnp.zeros((band, band), F32)
    upper = col > row
    near = row // small == col // small
    stricts = [jnp.where(upper, gram, zero) for gram in grams]

    at = lax.broadcasted_iota(jnp.int32, (small, band), 0)
    lane = lax.broadcasted_iota(jnp.int32, (small, band), 1)
    first = lane // small * small
    on_diagonal = lane - first == at
    none = jnp.zeros((small, band), F32)

    def gathered(value, index):
        return jnp.take_along_axis(value, index, axis=1)

    def side_by_side(value):
        parts = [value[i : i + small] for i in range(0, band, small)]
        return functools.reduce(jnp.add, parts)

    packed = [side_by_side(jnp.where(near, gram, zero)) for gram in grams]
    scales = [
        2.0 / jnp.sum(jnp.where(on_diagonal, p, none), axis=0, keepdims=True) for p in packed
    ]
    scaled = [
        jnp.where(lane - first > at, p, none) * s for p, s in zip(packed, scales)
    ]
    solved = [jnp.where(on_diagonal, 1.0, none) for _ in grams]
    for m in range(small - 1, 0, -1):
        columns = [gathered(s, first + m) for s in scaled]
        solved = [r - a * r[m : m + 1] for r, a in zip(solved, columns)]
    by_row = [gathered(jnp.broadcast_to(s, (small, band)), first + at) for s in scales]
    solved = [r * s for r, s in zip(solved, by_row)]
    found = [
        jnp.where(near, jnp.concatenate([r] * (band // small), axis=0), zero) for r in solved
    ]

    width = small
    while width < band:
        factor = 2 if band // width % 4 else 4
        wide = width * factor
        inside = (row // wide == col // wide) & (row // width != col // width)
        corners = [jnp.where(inside, strict, zero) for strict in stricts]
        powers = [multiply(a, b) for a, b in zip(found, corners)]
        firsts = [multiply(n, a) for n, a in zip(powers, found)]
        found = [a - b for a, b in zip(found, firsts)]
        if factor == 4:
            squares = [multiply(n, n) for n in powers]
            seconds = [multiply(n, a) for n, a in zip(squares, found)]
            found = [a + b for a, b in zip(found, seconds)]
        width = wide
    return found


def fast(a, b):
    return product(split(a), split(b))


def spread(w):
    band = w.shape[0]
    row = lax.broadcasted_iota(jnp.int32, (band, band), 0)
    col = lax.broadcasted_iota(jnp.int32, (band, band), 1)
    upper = col >= row
    zero = jnp.zeros((band, band), F32)
    return jnp.concatenate([jnp.where(upper, w, zero), jnp.where(upper, zero, w)], axis=1)


def own_blocks(sheared):
    v_parts = [split(spread(w)) for w in sheared]
    grams = [product(v, v, NT) for v in v_parts]
    factors = inverses(grams, fast)
    return [product(split(t), v) for t, v in zip(factors, v_parts)]


def paired_kernel(
    levels, n_z, slot_ref, eig_ref, wy_ref, out_ref,
    raw, vz, xin, xt, ops, flags,
    raw_recv, own_send, relay_send, core_recv, core_send, side_sem, local_sem,
):
    band = wy_ref.shape[1]
    chunks = eig_ref.shape[0] // band
    per_level = chunks // 2
    windows = 2 * per_level
    g = lax.axis_index("rows")
    c = lax.axis_index("cols")
    z, x, k = c // 4, (c // 2) % 2, c % 2
    flip_g, flip_x = 1 - 2 * g, 1 - 2 * x
    p1 = {"rows": 1 - g, "cols": c}
    p2 = {"rows": g, "cols": c + 2 * flip_x}
    p3 = {"rows": 1 - g, "cols": c + 2 * flip_x}
    core_partner = {"rows": g, "cols": c + 1 - 2 * k}
    row_partner = {"rows": 1 - g, "cols": c}

    side = jnp.where(z < n_z // 2, 1, n_z - 1)

    def near(i):
        return (z + side * (i + 1)) % n_z

    def upward(i):
        return i + (z <= i).astype(jnp.int32)

    def z_mate(zz):
        return {"rows": g, "cols": c + 4 * (zz - z)}

    own = g * levels + z * 2 + x
    opposite = (1 - g) * levels + z * 2 + 1 - x

    local_v = pltpu.make_async_copy(wy_ref.at[0], raw.at[own], local_sem.at[0])
    local_x = pltpu.make_async_copy(eig_ref, xin.at[g], local_sem.at[1])
    local_v.start()
    local_x.start()

    barrier = pltpu.get_barrier_semaphore()
    for d in range(1, n_z):
        pl.semaphore_signal(
            barrier, inc=1, device_id=z_mate((z + d) % n_z), device_id_type=MESH
        )
    for other in (p1, p2, p3, core_partner):
        pl.semaphore_signal(barrier, inc=1, device_id=other, device_id_type=MESH)

    level_row = lax.broadcasted_iota(jnp.int32, (levels, band), 0)
    tile = jnp.zeros((levels, band), F32)
    for level in range(levels):
        tile = jnp.where(level_row == level, slot_ref[0, 0, level].astype(F32), tile)
    flags[g] = tile
    xt[2 * chunks] = jnp.zeros((eig_ref.shape[1], band), F32)

    def remote(src, dst, send, recv, target):
        return pltpu.make_async_remote_copy(
            src_ref=src, dst_ref=dst, send_sem=send, recv_sem=recv,
            device_id=target, device_id_type=MESH,
        )

    def from_own(at, target):
        return remote(raw.at[own], raw.at[own], own_send.at[at], raw_recv.at[own], target)

    def to_z(zz):
        return from_own(zz, z_mate(zz))

    def relay(q, zz, way, target):
        return remote(raw.at[q], raw.at[q], relay_send.at[zz, way], raw_recv.at[q], target)

    def across(q):
        return remote(vz.at[k, q], vz.at[k, q], core_send.at[q], core_recv.at[q], core_partner)

    def flags_across():
        return remote(flags.at[g], flags.at[g], side_sem.at[0, 0], side_sem.at[1, 0], row_partner)

    def x_across():
        return remote(eig_ref, xin.at[g], side_sem.at[0, 1], side_sem.at[1, 1], row_partner)

    local_v.wait()
    pl.semaphore_wait(barrier, n_z + 3)

    @pl.when(k == 0)
    def _():
        from_own(n_z + 2, p3).start()

    for i in range(n_z - 1):
        to_z(near(i)).start()
    from_own(n_z, p1).start()
    from_own(n_z + 1, p2).start()
    flags_across().start()

    def factor(blocks):
        sheared = [pltpu.roll(jnp.transpose(raw[q]), 0, 1, stride=1, stride_axis=0) for q in blocks]
        for q, w, zed in zip(blocks, sheared, own_blocks(sheared)):
            vz[k, q, 0] = w
            vz[k, q, 1] = zed[:, :band]
            vz[k, q, 2] = zed[:, band:]
        for q in blocks:
            across(q).start()

    def plane(step):
        zz = jnp.where(step == 0, z, upward(step - 1))
        at = zz * 2 + x
        mine = g * levels + at
        across_y = (1 - g) * levels + at
        across_x = g * levels + at + flip_x
        across_both = (1 - g) * levels + at + flip_x
        blocks = [mine, across_y, across_x, across_both]

        @pl.when((step == 0) & (k == 0))
        def _():
            relay(across_both, 0, 0, p1).wait_recv()
            for d in range(n_z - 1, 0, -1):
                far = (z + d) % n_z
                relay(opposite, far, 2, z_mate(far)).start()

        @pl.when((step == 0) & (k == 1))
        def _():
            relay(across_y, 0, 0, p1).wait_recv()
            relay(across_y, z, 2, p2).start()

        @pl.when(step == 0)
        def _():
            for i in range(n_z - 1):
                far = upward(i)
                q = g * levels + far * 2 + x
                relay(q, far, 0, p1).wait_recv()
                relay(q, far, 0, p1).start()
                relay(q, far, 1, p2).start()
            x_across().start()

        @pl.when(k == 0)
        def _():
            relay(across_y, 0, 0, p1).wait_recv()

        @pl.when((step > 0) | (k == 1))
        def _():
            relay(across_both, 0, 0, p1).wait_recv()

        relay(across_x, 0, 0, p1).wait_recv()

        @pl.when((step == 0) & (k == 1))
        def _():
            for i in range(n_z - 1):
                far = upward(i)
                q = (1 - g) * levels + far * 2 + x
                relay(q, far, 0, p1).wait_recv()
                relay(q, far, 2, p2).start()

        return blocks


    def ready(level, base):
        for r in range(2):
            q = r * levels + level
            first = flags[r, pl.ds(level, 1), :] < 0.5
            a, b = vz[0, q], vz[1, q]
            for h, w in enumerate((jnp.where(first, a, b), jnp.where(first, b, a))):
                v = split(spread(w[0]))
                zed = split(jnp.concatenate([w[1], w[2]], axis=1))
                at = base + r * per_level + h
                ops[at, 0], ops[at, 1] = zed
                ops[at, 2], ops[at, 3] = v

    def reflected(base, shift):
        pairs = [
            jnp.concatenate([xt[2 * i + shift], xt[2 * i + shift + 1]], axis=1)
            for i in range(windows)
        ]
        halves = [split(pair) for pair in pairs]
        projected = [
            split(product(h, (ops[base + i, 0], ops[base + i, 1]), NT))
            for i, h in enumerate(halves)
        ]
        for i, (pair, y) in enumerate(zip(pairs, projected)):
            new = pair - product(y, (ops[base + i, 2], ops[base + i, 3]))
            xt[2 * i + shift] = new[:, :band]
            if 2 * i + shift + 1 < 2 * chunks:
                xt[2 * i + shift + 1] = new[:, band:]

    def both_levels(at):
        @pl.when(at == 0)
        def _():
            local_x.wait()
            x_across().wait_recv()
            flags_across().wait_recv()
            for r in range(2):
                for i in range(chunks):
                    xt[r * chunks + i] = jnp.transpose(xin[r, i * band : (i + 1) * band, :])

        for i in range(2):
            for r in range(2):
                across(r * levels + 2 * at + i).wait_recv()
        ready(2 * at, 0)
        ready(2 * at + 1, windows)
        reflected(0, 0)
        reflected(windows, 1)

    def turn(step, carry):
        @pl.when(step < n_z // 2)
        def _():
            factor(plane(2 * step) + plane(2 * step + 1))

        @pl.when(step >= n_z // 2 - 1)
        def _():
            both_levels(step - (n_z // 2 - 1))

        return carry

    lax.fori_loop(0, n_z + n_z // 2 - 1, turn, 0)

    for i in range(chunks):
        out_ref[i * band : (i + 1) * band, :] = jnp.transpose(xt[g * chunks + i])

    for zz in range(n_z):
        q = own + 2 * (zz - z)

        @pl.when(zz != z)
        def _():
            to_z(zz).wait_send()
            relay(q, zz, 0, p1).wait_send()
            relay(q, zz, 1, p2).wait_send()

        @pl.when((zz != z) | (k == 1))
        def _():
            relay(q, zz, 2, p2).wait_send()

    from_own(n_z, p1).wait_send()
    from_own(n_z + 1, p2).wait_send()

    @pl.when(k == 0)
    def _():
        from_own(n_z + 2, p3).wait_send()

    flags_across().wait_send()
    x_across().wait_send()
    for q in range(2 * levels):
        across(q).wait_send()


def paired(n_cols, eigvecs, wy_packed, slot_block):
    band = wy_packed.shape[1]
    rows, cols = eigvecs.shape
    levels, per_level = slot_block.shape[1:]
    n_z = n_cols // 4
    chunks = rows // band
    assert n_cols == levels * per_level and 2 * n_z == levels
    assert wy_packed.shape[0] == 1 and per_level == 2 and chunks == 2 * per_level
    anywhere = pl.BlockSpec(memory_space=pl.ANY)
    dma = pltpu.SemaphoreType.DMA
    return pl.pallas_call(
        functools.partial(paired_kernel, levels, n_z),
        out_shape=jax.ShapeDtypeStruct(eigvecs.shape, F32),
        in_specs=[pl.BlockSpec(memory_space=pltpu.SMEM), anywhere, anywhere],
        out_specs=pl.BlockSpec(memory_space=pltpu.VMEM),
        scratch_shapes=[
            pltpu.VMEM((2 * levels, band, band), F32),
            pltpu.VMEM((2, 2 * levels, 3, band, band), F32),
            pltpu.VMEM((2, rows, cols), F32),
            pltpu.VMEM((2 * chunks + 1, cols, band), F32),
            pltpu.VMEM((4 * per_level, 4, band, 2 * band), BF16),
            pltpu.VMEM((2, levels, band), F32),
            dma((2 * levels,)),
            dma((n_z + 3,)),
            dma((n_z, 3)),
            dma((2 * levels,)),
            dma((2 * levels,)),
            dma((2, 2)),
            dma((2,)),
        ],
        compiler_params=pltpu.CompilerParams(collective_id=0, has_side_effects=True),
    )(jnp.swapaxes(slot_block, 1, 2), eigvecs, wy_packed)


def kernel(
    levels, n_rows, n_z, slot_ref, eig_ref, wy_ref, out_ref,
    wg, xt, ops, half_send, above, up_send, up_recv, down_send, down_recv,
    recv_sem, send_sem, own_sem, up_sem, down_sem, half_sem, side_sem,
):
    band = wy_ref.shape[1]
    chunks = eig_ref.shape[0] // band
    per_level = chunks // 2
    rounds = levels // 2
    g = lax.axis_index("rows")
    c = lax.axis_index("cols")
    z, x, k = c // 4, (c // 2) % 2, c % 2
    x_partner = z * 4 + (1 - x) * 2 + k
    core_partner = z * 4 + x * 2 + (1 - k)
    z_mates = [((z + d) % n_z) * 4 + x * 2 + k for d in range(1, n_z)]
    has_above = g > 0
    has_below = g < n_rows - 1

    barrier = pltpu.get_barrier_semaphore()
    for other in z_mates + [x_partner, core_partner]:
        pl.semaphore_signal(barrier, inc=1, device_id={"cols": other}, device_id_type=MESH)

    @pl.when(has_above)
    def _():
        pl.semaphore_signal(barrier, inc=1, device_id={"rows": g - 1}, device_id_type=MESH)

    @pl.when(has_below)
    def _():
        pl.semaphore_signal(barrier, inc=1, device_id={"rows": g + 1}, device_id_type=MESH)

    def block_copy(block, target, sem):
        return pltpu.make_async_remote_copy(
            src_ref=wg.at[block],
            dst_ref=wg.at[block],
            send_sem=sem,
            recv_sem=recv_sem.at[block],
            device_id={"cols": target},
            device_id_type=MESH,
        )

    def to_x(zz, xx):
        return block_copy(zz * 4 + xx * 2 + k, x_partner, send_sem.at[zz * 2 + xx, 0])

    def to_core(zz, xx):
        return block_copy(zz * 4 + xx * 2 + k, core_partner, send_sem.at[zz * 2 + xx, 1])

    def to_z(zz):
        return block_copy(c, zz * 4 + x * 2 + k, own_sem.at[zz])

    def relay_z(zz):
        @pl.when(z != zz)
        def _():
            to_x(zz, x).wait_recv()
            to_x(zz, x).start()
            to_core(zz, x).start()

    def relay_x(zz):
        to_core(zz, 1 - x).wait_recv()
        to_core(zz, 1 - x).start()

    def wait_core(zz):
        for xx in range(2):
            block_copy(zz * 4 + xx * 2 + 1 - k, core_partner, send_sem.at[0, 0]).wait_recv()

    def row_copy(src, dst, sem, at, target):
        return pltpu.make_async_remote_copy(
            src_ref=src.at[at],
            dst_ref=dst.at[at],
            send_sem=sem.at[0, at],
            recv_sem=sem.at[1, at],
            device_id={"rows": target},
            device_id_type=MESH,
        )

    def go_up(at):
        return row_copy(up_send, up_recv, up_sem, at, g - 1)

    def go_down(at):
        return row_copy(down_send, down_recv, down_sem, at, g + 1)

    half = band // 2

    def half_down(at):
        return pltpu.make_async_remote_copy(
            src_ref=half_send.at[at],
            dst_ref=above.at[at, pl.ds(k * half, half)],
            send_sem=half_sem.at[0, at],
            recv_sem=half_sem.at[1, at],
            device_id={"rows": g + 1},
            device_id_type=MESH,
        )

    def half_side(at):
        return pltpu.make_async_remote_copy(
            src_ref=above.at[at, pl.ds(k * half, half)],
            dst_ref=above.at[at, pl.ds(k * half, half)],
            send_sem=side_sem.at[0, at],
            recv_sem=side_sem.at[1, at],
            device_id={"cols": core_partner},
            device_id_type=MESH,
        )

    def send_half(at):
        level = 2 * at + 1
        first = slot_ref[0, per_level - 1, level] == 0
        rows = pl.ds(k * half, half)
        half_send[at] = jnp.where(
            first, wg[level * per_level, rows], wg[level * per_level + 1, rows]
        )
        half_down(at).start()

    wg[c] = pltpu.roll(jnp.transpose(wy_ref[0]), 0, 1, stride=1, stride_axis=0)
    pl.semaphore_wait(
        barrier, n_z + 1 + has_above.astype(jnp.int32) + has_below.astype(jnp.int32)
    )
    to_x(z, x).start()
    to_core(z, x).start()
    for far in range(n_z - 1, -1, -1):
        @pl.when((far != z) & ((far < z) | (z < 2)))
        def _():
            to_z(far).start()

    @pl.when(jnp.logical_not(has_above))
    def _():
        above[...] = jnp.zeros_like(above)
        down_recv[...] = jnp.zeros_like(down_recv)

    @pl.when(jnp.logical_not(has_below))
    def _():
        up_recv[...] = jnp.zeros_like(up_recv)

    for i in range(chunks):
        xt[i] = jnp.transpose(eig_ref[i * band : (i + 1) * band, :])

    def chosen(level, h):
        first = slot_ref[0, h, level] == 0
        return jnp.where(first, wg[level * per_level], wg[level * per_level + 1])

    def prepare(sheared, places):
        v_parts = [split(spread(w)) for w in sheared]
        grams = [product(v, v, NT) for v in v_parts]
        factors = inverses(grams, fast)
        for place, v, t in zip(places, v_parts, factors):
            z_parts = split(product(split(t), v))
            ops[place, 0] = z_parts[0]
            ops[place, 1] = z_parts[1]
            ops[place, 2] = v[0]
            ops[place, 3] = v[1]

    def reflected(places, pairs):
        halves = [split(pair) for pair in pairs]
        projected = [
            split(product(x, (ops[p, 0], ops[p, 1]), NT)) for p, x in zip(places, halves)
        ]
        return [
            pair - product(y, (ops[p, 2], ops[p, 3]))
            for p, y, pair in zip(places, projected, pairs)
        ]

    def window(top, bottom):
        return jnp.concatenate([top, bottom], axis=1)

    relay_z(0)

    @pl.when(z >= 2)
    def _():
        for far in range(n_z - 1, 2, -1):
            @pl.when(far > z)
            def _():
                to_z(far).start()

    relay_x(0)
    wait_core(0)

    @pl.when(has_below)
    def _():
        send_half(0)

    relay_z(1)
    prepare([chosen(0, 0), chosen(0, 1)], [3, 4])

    def both_levels(at, carry):
        @pl.when(has_above)
        def _():
            half_down(at).wait_recv()
            half_side(at).start()

        upper_new, lower_new = reflected([3, 4], [window(xt[0], xt[1]), window(xt[2], xt[3])])
        xt[0], xt[1] = upper_new[:, :band], upper_new[:, band:]
        xt[2], xt[3] = lower_new[:, :band], lower_new[:, band:]

        @pl.when(has_above)
        def _():
            up_send[at] = xt[0]
            go_up(at).start()

        @pl.when(has_below)
        def _():
            down_send[at] = xt[chunks - 1]
            go_down(at).start()

        @pl.when(at < rounds - 1)
        def _():
            relay_x(at + 1)
            wait_core(at + 1)

            @pl.when(has_below)
            def _():
                send_half(at + 1)

        @pl.when(at < rounds - 2)
        def _():
            relay_z(at + 2)

        @pl.when(has_above)
        def _():
            half_side(at).wait_recv()

        odd, even = 2 * at + 1, (2 * at + 2) % levels
        prepare(
            [chosen(odd, 0), chosen(odd, 1), above[at], chosen(even, 0), chosen(even, 1)],
            [0, 1, 2, 3, 4],
        )

        @pl.when(has_below)
        def _():
            go_up(at).wait_recv()

        @pl.when(has_above)
        def _():
            go_down(at).wait_recv()

        middle, last, first = reflected(
            [0, 1, 2],
            [
                window(xt[1], xt[2]),
                window(xt[chunks - 1], up_recv[at]),
                window(down_recv[at], xt[0]),
            ],
        )
        xt[1], xt[2] = middle[:, :band], middle[:, band:]
        xt[chunks - 1] = last[:, :band]
        xt[0] = jnp.where(has_above, first[:, band:], xt[0])
        return carry

    lax.fori_loop(0, rounds, both_levels, 0)

    for i in range(chunks):
        out_ref[i * band : (i + 1) * band, :] = jnp.transpose(xt[i])

    for zz in range(n_z):
        @pl.when(z != zz)
        def _():
            to_z(zz).wait_send()

    for zz in range(n_z):
        to_x(zz, x).wait_send()
        for xx in range(2):
            to_core(zz, xx).wait_send()
    for at in range(rounds):
        @pl.when(has_above)
        def _():
            go_up(at).wait_send()
            half_side(at).wait_send()

        @pl.when(has_below)
        def _():
            go_down(at).wait_send()
            half_down(at).wait_send()


def per_device(n_rows, n_cols, eigvecs, wy_packed, slot_block):
    if n_rows == 2:
        return paired(n_cols, eigvecs, wy_packed, slot_block)
    band = wy_packed.shape[1]
    rows, cols = eigvecs.shape
    levels, per_level = slot_block.shape[1:]
    n_z = n_cols // 4
    rounds = levels // 2
    assert n_cols == levels * per_level and n_z == rounds
    assert wy_packed.shape[0] == 1 and per_level == 2 and rows == 4 * band
    blocks = pltpu.VMEM((rounds, band, band), F32)
    slots = pltpu.VMEM((rounds, cols, band), F32)
    vmem = pl.BlockSpec(memory_space=pltpu.VMEM)
    in_order = pltpu.SemaphoreType.DMA((2, rounds))
    return pl.pallas_call(
        functools.partial(kernel, levels, n_rows, n_z),
        out_shape=jax.ShapeDtypeStruct(eigvecs.shape, F32),
        in_specs=[pl.BlockSpec(memory_space=pltpu.SMEM), vmem, vmem],
        out_specs=vmem,
        scratch_shapes=[
            pltpu.VMEM((n_cols, band, band), F32),
            pltpu.VMEM((rows // band, cols, band), F32),
            pltpu.VMEM((5, 4, band, 2 * band), BF16),
            pltpu.VMEM((rounds, band // 2, band), F32),
            blocks,
            slots,
            slots,
            slots,
            slots,
            pltpu.SemaphoreType.DMA((n_cols,)),
            pltpu.SemaphoreType.DMA((n_cols // 2, 2)),
            pltpu.SemaphoreType.DMA((n_z,)),
            in_order,
            in_order,
            in_order,
            in_order,
        ],
        compiler_params=pltpu.CompilerParams(collective_id=0, has_side_effects=True),
    )(jnp.swapaxes(slot_block, 1, 2), eigvecs, wy_packed)


def solution(mesh):
    placed = (P("rows", "cols"), P(("rows", "cols"), None, None), P("rows", None, None))
    return jax.shard_map(
        functools.partial(per_device, mesh.shape["rows"], mesh.shape["cols"]),
        mesh=mesh, in_specs=placed, out_specs=P("rows", "cols"), check_vma=False,
    )
```
